256 devices in a mesh: leaf: 64 (over z, y, core), rhs: 4 (over x).
Axes of the slice: x: 4, y: 4, z: 8, core: 2. Of those that a mesh axis runs over, the one named last changes fastest.
Arguments:
- densities: bfloat16 [64, 262144], P('rhs', 'leaf'), may hold values from -6 to 6
- bases: float32 [32, 262144], P(None, 'leaf'), may hold values from -0.5 to 0.5
- near_blocks: bfloat16 [2048, 8, 128, 128], P('leaf', 'rhs'), may hold values from -0.1875 to 0.1875
- near_src: int32 [2048, 8], P('leaf', 'rhs'), may hold values from 0 to 55, as said below
- send_leaf: int32 [64, 6, 4], replicated, may hold values from -1 to 31, as said below
- far_src: int32 [2048, 8], P('leaf'), may hold values from 0 to 31
- leaf_coupling: float32 [2048, 8, 32, 32], P('leaf'), may hold values from -0.375 to 0.375
- local_transfer: float32 [64, 64, 32, 32], P('leaf'), may hold values from -0.75 to 0.75
- upper_transfer: float32 [128, 32, 32], replicated, may hold values from -0.75 to 0.75
- up_coupling: float32 [128, 3, 32, 32], replicated, may hold values from -8 to 8
Outputs:
- product: float32 [64, 262144], P('rhs', 'leaf')
The draws below stay inside these ranges and needn't reach their ends.
Inputs may be any that keep to these rules, and one draw needn't show every extreme that they name: `send_leaf`: entry [e, j, c] is a leaf of device e (local index) whose panel e sends to its face neighbour e + o_j, or -1. Only existing face neighbours receive; the leaves of [e, j] are distinct and come before the -1 entries; every device sends exactly 4 leaves to at least one neighbour, among them its leaf 32 - 1, and exactly 4 to its neighbour at offset -s*s where that exists. `near_src`: A slot of the owner's panel buffer: below 32 a leaf of the same device, else slot 32 + j * 4 + c. It never names an empty slot, and every filled slot is named by some block of the device.
All inputs are finite; a program needn't handle non-finite values.
Results may differ from the reference program's by a relative error of at most 0.0003.
Values may be sent and summed in bfloat16 or wider, within the bound.
A program may use at most 128 MiB of HBM per device.

```python
import jax
import jax.numpy as jnp
from jax import lax

LEAF_SIZE = 128
RANK = 32
RHS = 64
NEAR = 8
FAR = 8
CAP = 4
LEAVES_DEV = 32
LEAVES = 2048
POINTS = 262144
N_LEAF = 64


def cube_side_drawn(device_count):
    return max((edge_len for edge_len in range(1, 65) if edge_len ** 3 <= device_count))


def routing_tables(key):
    side_len = cube_side_drawn(N_LEAF)
    device_ids = jnp.arange(N_LEAF, dtype=jnp.int32)
    coord_x = device_ids % side_len
    coord_y = device_ids // side_len % side_len
    coord_z = device_ids // (side_len * side_len)
    exists = jnp.stack([coord_x < side_len - 1, coord_x > 0, coord_y < side_len - 1, coord_y > 0, coord_z < side_len - 1, coord_z > 0], axis=1)
    base_key = jax.random.fold_in(key, 4242)
    key_count, key_force, key_order, key_pick = jax.random.split(base_key, 4)
    counts = jax.random.randint(key_count, (N_LEAF, 6), 1, CAP + 1)
    forced = jax.random.randint(key_force, (N_LEAF,), 0, 6)
    forced_ok = jnp.take_along_axis(exists, forced[:, None], axis=1)[:, 0]
    chosen_dir = jnp.where(forced_ok, forced, forced ^ 1)
    counts = jnp.where(jnp.arange(6)[None, :] == chosen_dir[:, None], CAP, counts)
    counts = jnp.where(jnp.arange(6)[None, :] == 5, CAP, counts)
    counts = jnp.where(exists, counts, 0)
    scores = jax.random.randint(key_order, (N_LEAF, 6, LEAVES_DEV), 0, 1 << 20) * LEAVES_DEV + jnp.arange(LEAVES_DEV)
    top_leaf = (jnp.arange(6)[None, :, None] == chosen_dir[:, None, None]) & (jnp.arange(LEAVES_DEV)[None, None, :] == LEAVES_DEV - 1)
    scores = jnp.where(top_leaf, -1, scores)
    order = jnp.argsort(scores, axis=-1)[..., :CAP].astype(jnp.int32)
    send_leaf = jnp.where(jnp.arange(CAP)[None, None, :] < counts[..., None], order, -1).astype(jnp.int32)
    offsets = jnp.array([1, -1, side_len, -side_len, side_len * side_len, -side_len * side_len], dtype=jnp.int32)
    senders = jnp.clip(device_ids[:, None] - offsets[None, :], 0, N_LEAF - 1)
    sender_counts = counts[senders, jnp.arange(6)[None, :]]
    incoming_ok = exists[:, jnp.array([1, 0, 3, 2, 5, 4])]
    live = incoming_ok[..., None] & (jnp.arange(CAP)[None, None, :] < sender_counts[..., None])
    live_flat = live.reshape(N_LEAF, 6 * CAP)
    rank_keys = jnp.where(live_flat, 0, 1) * (6 * CAP) + jnp.arange(6 * CAP)[None, :]
    remote_sorted = (jnp.argsort(rank_keys, axis=1) + LEAVES_DEV).astype(jnp.int32)
    live_total = jnp.sum(live_flat.astype(jnp.int32), axis=1)
    pool_size = live_total + LEAVES_DEV
    pick_total = LEAVES_DEV * (NEAR - 1)
    pick_scores = jax.random.randint(key_pick, (N_LEAF, pick_total), 0, 1 << 20) * pick_total + jnp.arange(pick_total)[None, :]
    pick_perm = jnp.argsort(pick_scores, axis=1).astype(jnp.int32)
    position = pick_perm % pool_size[:, None]
    remote_value = jnp.take_along_axis(remote_sorted, jnp.clip(position, 0, 6 * CAP - 1), axis=1)
    local_value = position - live_total[:, None]
    chosen_value = jnp.where(position < live_total[:, None], remote_value, local_value)
    chosen_value = chosen_value.reshape(N_LEAF, LEAVES_DEV, NEAR - 1)
    self_slot = jnp.broadcast_to(jnp.arange(LEAVES_DEV, dtype=jnp.int32)[None, :, None], (N_LEAF, LEAVES_DEV, 1))
    near_src = jnp.concatenate([self_slot, chosen_value], axis=2).reshape(LEAVES, NEAR).astype(jnp.int32)
    return (send_leaf, near_src)


def draw_send_leaf(key, part):
    return routing_tables(key)[0]


def draw_near_src(key, part):
    return routing_tables(key)[1]


def draw_up_coupling(key, part):
    leaf_bits = int(N_LEAF).bit_length() - 1
    subtree_bits = int(LEAVES_DEV).bit_length() - 1
    node_ids = jnp.arange(2 * N_LEAF, dtype=jnp.int32)
    level_of = jnp.zeros((2 * N_LEAF,), jnp.int32)
    for level_bit in range(1, leaf_bits + 1):
        level_of = level_of + (node_ids >= 1 << level_bit).astype(jnp.int32)
    halvings = (leaf_bits - level_of + subtree_bits).astype(jnp.float32)
    spread = jnp.exp2(0.5 * halvings) / jnp.sqrt(jnp.float32(3 * RANK))
    draw_key = jax.random.fold_in(key, 5151)
    raw_values = jax.random.normal(draw_key, (2 * N_LEAF, 3, RANK, RANK), jnp.float32)
    return jnp.clip(raw_values * spread[:, None, None, None], -8.0, 8.0)


def with_ends(entries, own_key, smallest, high):
    place = [jax.random.randint(jax.random.fold_in(own_key, axis), (), 0, length) for axis, length in enumerate(entries.shape)]
    main_axis = entries.shape.index(max(entries.shape))
    beside = place[:main_axis] + [(place[main_axis] + 1) % entries.shape[main_axis]] + place[main_axis + 1:]
    return entries.at[tuple(place)].set(smallest).at[tuple(beside)].set(high)


def block_scale(own_key, extent, cuts, low, largest):
    factor_of, own = 1.0, jax.random.fold_in(own_key, 6)
    for dim, parts in cuts:
        draws = jnp.exp(jax.random.uniform(jax.random.fold_in(own, dim), (parts,), jnp.float32, low / len(cuts), largest / len(cuts)))
        factor_of = factor_of * jnp.repeat(draws, extent[dim] // parts).reshape([-1 if axis == dim else 1 for axis in range(len(extent))])
    return factor_of


def noise(stream_key, extent, deviation, limit, cuts=(), kind=jnp.bfloat16):
    factor_of = block_scale(stream_key, extent, cuts, -0.22, 0.18) if cuts else 1.0
    values = jax.random.normal(stream_key, extent, jnp.float32) * deviation * factor_of
    return jnp.minimum(jnp.maximum(values, -limit), limit).astype(kind)


def setup_inputs(seed: int = 0) -> dict:
    splits = jax.random.split(jax.random.key(seed), 11)
    densities = noise(splits[0], (RHS, POINTS), 1.0, 6.0, ((0, 4), (1, 64)))
    bases = noise(splits[1], (RANK, POINTS), LEAF_SIZE ** -0.5, 0.5, ((1, 64),), jnp.float32)
    near_blocks = noise(splits[2], (LEAVES, NEAR, LEAF_SIZE, LEAF_SIZE), (LEAF_SIZE * NEAR) ** -0.5, 0.1875, ((0, 64), (1, 4)))
    near_src = draw_near_src(jax.random.fold_in(splits[10], 71), 0)
    send_leaf = draw_send_leaf(jax.random.fold_in(splits[10], 71), 0)
    far_src = with_ends(jax.random.randint(splits[5], (LEAVES, FAR), 0, LEAVES_DEV), jax.random.fold_in(splits[5], 1), 0, LEAVES_DEV - 1).astype(jnp.int32)
    leaf_coupling = noise(splits[6], (LEAVES, FAR, RANK, RANK), (RANK * FAR) ** -0.5, 0.375, ((0, 64),), jnp.float32)
    local_transfer = noise(splits[7], (N_LEAF, 2 * LEAVES_DEV, RANK, RANK), (2 * RANK) ** -0.5, 0.75, ((0, 64),), jnp.float32)
    upper_transfer = noise(splits[8], (2 * N_LEAF, RANK, RANK), (2 * RANK) ** -0.5, 0.75, (), jnp.float32)
    up_coupling = draw_up_coupling(jax.random.fold_in(splits[10], 71), 0)
    return {"densities": densities, "bases": bases, "near_blocks": near_blocks, "near_src": near_src, "send_leaf": send_leaf, "far_src": far_src, "leaf_coupling": leaf_coupling, "local_transfer": local_transfer, "upper_transfer": upper_transfer, "up_coupling": up_coupling}


TOP_PREC = lax.Precision.HIGHEST
FACE_SIGNS = ((1, 0), (-1, 0), (1, 1), (-1, 1), (1, 2), (-1, 2))


def cube_side(device_count):
    return max(edge_len for edge_len in range(1, 65) if edge_len ** 3 <= device_count)


def face_offsets(device_count):
    side_len = cube_side(device_count)
    return [face_sign * side_len ** axis_pos for face_sign, axis_pos in FACE_SIGNS]


def lift_pairs(child_coef, child_maps):
    lifted = jnp.einsum('...nrs,...nqr->...nqs', child_maps, child_coef, precision=TOP_PREC)
    return lifted[..., 0::2, :, :] + lifted[..., 1::2, :, :]


def apply_maps(node_maps, coef_rows):
    return jnp.einsum('...nrs,...nqs->...nqr', node_maps, coef_rows, precision=TOP_PREC)


def couple_level(coef_level, maps_level):
    level_width = coef_level.shape[0]
    even_node = (jnp.arange(level_width) % 2) == 0
    padded = jnp.pad(coef_level, ((3, 3), (0, 0), (0, 0)))
    minus_two = padded[1:level_width + 1]
    plus_two = padded[5:level_width + 5]
    third_node = jnp.where(even_node[:, None, None], padded[6:level_width + 6], padded[0:level_width])
    first_terms = apply_maps(maps_level[:, 0], minus_two) + apply_maps(maps_level[:, 1], plus_two)
    return first_terms + apply_maps(maps_level[:, 2], third_node)


def upper_tree(roots, upper_transfer, up_coupling):
    node_total = roots.shape[0]
    coef_levels = {node_total: roots}
    level_width = node_total
    while level_width > 4:
        coef_levels[level_width // 2] = lift_pairs(coef_levels[level_width], upper_transfer[level_width:2 * level_width])
        level_width = level_width // 2
    level_field = couple_level(coef_levels[4], up_coupling[4:8])
    level_width = 4
    while level_width < node_total:
        level_width = level_width * 2
        coupled = couple_level(coef_levels[level_width], up_coupling[level_width:2 * level_width])
        level_field = coupled + apply_maps(upper_transfer[level_width:2 * level_width], jnp.repeat(level_field, 2, axis=0))
    return level_field


def slot_table(send_leaf):
    offsets = face_offsets(N_LEAF)
    device_ids = jnp.arange(N_LEAF, dtype=jnp.int32)
    leaf_ids = []
    live_parts = []
    for direction in range(6):
        sender = device_ids - offsets[direction]
        inside = (sender >= 0) & (sender < N_LEAF)
        clipped = jnp.clip(sender, 0, N_LEAF - 1).astype(jnp.int32)
        sent_leaf = send_leaf[clipped, direction, :]
        live_parts.append(inside[:, None] & (sent_leaf >= 0))
        leaf_ids.append(clipped[:, None] * LEAVES_DEV + jnp.maximum(sent_leaf, 0))
    local_ids = device_ids[:, None] * LEAVES_DEV + jnp.arange(LEAVES_DEV, dtype=jnp.int32)[None, :]
    local_live = jnp.ones(local_ids.shape, dtype=jnp.bool_)
    all_ids = jnp.concatenate([local_ids] + leaf_ids, axis=1).astype(jnp.int32)
    all_live = jnp.concatenate([local_live] + live_parts, axis=1)
    return all_ids, all_live


def reference(densities, bases, near_blocks, near_src, send_leaf, far_src, leaf_coupling, local_transfer, upper_transfer, up_coupling):
    all_ids, all_live = slot_table(send_leaf)
    panels_all = densities.reshape(RHS, LEAVES, LEAF_SIZE)
    blocks_dev = near_blocks.reshape(N_LEAF, LEAVES_DEV, NEAR, LEAF_SIZE, LEAF_SIZE)
    sources_dev = near_src.reshape(N_LEAF, LEAVES_DEV, NEAR)

    def near_device(packed):
        blocks, sources, id_row, live_row = packed
        chosen = jnp.take(id_row, sources, axis=0)
        alive = jnp.take(live_row, sources, axis=0)
        picked = jnp.take(panels_all, chosen, axis=1)
        picked = jnp.where(alive[None, :, :, None], picked, jnp.zeros_like(picked))
        return jnp.einsum('tkij,qtkj->qti', blocks.astype(jnp.float32), picked.astype(jnp.float32), precision=TOP_PREC)

    near_parts = lax.map(near_device, (blocks_dev, sources_dev, all_ids, all_live))
    near_field = jnp.transpose(near_parts, (1, 0, 2, 3)).reshape(RHS, POINTS)

    basis_view = bases.reshape(RANK, LEAVES, LEAF_SIZE)
    leaf_coef = jnp.einsum('rti,qti->tqr', basis_view, panels_all.astype(jnp.float32), precision=TOP_PREC)
    leaf_coef = leaf_coef.reshape(N_LEAF, LEAVES_DEV, RHS, RANK)
    coef_levels = {LEAVES_DEV: leaf_coef}
    level_width = LEAVES_DEV
    while level_width > 1:
        coef_levels[level_width // 2] = lift_pairs(coef_levels[level_width], local_transfer[:, level_width:2 * level_width])
        level_width = level_width // 2
    root_field = upper_tree(coef_levels[1][:, 0], upper_transfer, up_coupling)

    far_dev = far_src.reshape(N_LEAF, LEAVES_DEV, FAR)
    picked_coef = jax.vmap(lambda coef_rows, far_index: jnp.take(coef_rows, far_index, axis=0))(leaf_coef, far_dev)
    coupling_view = leaf_coupling.reshape(N_LEAF, LEAVES_DEV, FAR, RANK, RANK)
    leaf_local = jnp.einsum('...tjrs,...tjqs->...tqr', coupling_view, picked_coef, precision=TOP_PREC)

    level_field = root_field[:, None]
    level_width = 1
    while level_width < LEAVES_DEV:
        level_width = level_width * 2
        level_field = apply_maps(local_transfer[:, level_width:2 * level_width], jnp.repeat(level_field, 2, axis=1))
    leaf_field = level_field + leaf_local
    far_part = jnp.einsum('rti,tqr->qti', basis_view, leaf_field.reshape(LEAVES, RHS, RANK), precision=TOP_PREC)
    return near_field + far_part.reshape(RHS, POINTS)
```

```python
import functools

import jax
import jax.numpy as jnp
from jax import lax
from jax.experimental import pallas as pl
from jax.experimental.pallas import tpu as pltpu
from jax.sharding import PartitionSpec as P

F32 = jnp.float32
BF16 = jnp.bfloat16
MESH = pl.DeviceIdType.MESH
LEAVES = 32
WIDTH = 128
COLS = 16
NLEAF = 64
NRHS = 4
SLOTS = 56
FACES = (1, -1, 4, -4, 16, -16)
GREET = (1, -1, 2, -2, 3, -3, 4, -4, 6, -6, 8, -8, 12, -12, 16, -16, 24, -24, 32)
CHUNKS = 4
CHUNK = LEAVES // CHUNKS


def dot_nn(a, b):
    return lax.dot_general(a, b, (((1,), (0,)), ((), ())), preferred_element_type=F32)


def dot_nt(a, b):
    return lax.dot_general(a, b, (((1,), (1,)), ((), ())), preferred_element_type=F32)


def halves(x):
    high = x.astype(BF16)
    return high, (x - high.astype(F32)).astype(BF16)


def lane_group(shape):
    return lax.broadcasted_iota(jnp.int32, shape, len(shape) - 1) // 32


def coef_form(r):
    group = lane_group(r.shape)
    high = r.astype(BF16).astype(F32)
    return jnp.where(group % 2 == 0, high, r - high).astype(BF16)


def unfold(tile):
    group = lane_group(tile.shape)
    turned = [tile] + [pltpu.roll(tile, 32 * k, 1) for k in (1, 2, 3)]
    rows = []
    for b in range(4):
        pick = [turned[(g - b) % 4] for g in range(4)]
        rows.append(
            jnp.where(
                group < 2,
                jnp.where(group == 0, pick[0], pick[1]),
                jnp.where(group == 2, pick[2], pick[3]),
            )
        )
    return jnp.concatenate(rows, axis=0)


def rows_form(high, low):
    return jnp.concatenate([high, high, low, low], axis=0)


def lanes_form(m):
    high = m.astype(BF16).astype(F32)
    v = jnp.where(lane_group(m.shape) < 2, high, m - high).astype(BF16)
    return jnp.concatenate([v] * 4, axis=0)


def kernel(
    dens,
    bases,
    blocks,
    nsrc,
    sleaf,
    fsrc,
    coup,
    loc_t,
    up_t,
    up_c,
    out,
    own,
    buf,
    stage,
    bas_v,
    blk_v,
    cpl_v,
    loc_v,
    upt_v,
    upc_v,
    ef,
    uf,
    cf,
    e_hi,
    e_lo,
    e_v,
    b_hi,
    b_lo,
    f_rep,
    x_up,
    x_dn,
    ll,
    acc,
    lvl,
    lrecv,
    part,
    rbuf,
    own_sem,
    loc_sem,
    xs_sem,
    xr_sem,
    hs_sem,
    hr_sem,
    ys_sem,
    yr_sem,
    ls_sem,
    lr_sem,
    rs_sem,
    rr_sem,
):
    d = lax.axis_index("leaf")
    me = lax.axis_index("rhs")
    my_rows = pl.ds(pl.multiple_of(me * COLS, COLS), COLS)

    def leaf_at(offset):
        return lax.rem(d + (offset + 2 * NLEAF), NLEAF)

    def rhs_at(offset):
        return lax.rem(me + offset, NRHS)

    barrier = pltpu.get_barrier_semaphore()
    for offset in (1, 2, 3):
        pl.semaphore_signal(barrier, inc=1, device_id={"rhs": rhs_at(offset)}, device_id_type=MESH)
    for offset in GREET:
        pl.semaphore_signal(
            barrier, inc=1, device_id={"leaf": leaf_at(offset)}, device_id_type=MESH
        )

    def own_copy(k):
        return pltpu.make_async_copy(
            dens.at[:, pl.ds(pl.multiple_of(k * WIDTH, WIDTH), WIDTH)], own.at[k], own_sem.at[k]
        )

    pairs = (
        (bases, bas_v),
        (loc_t, loc_v),
        (blocks, blk_v),
        (up_t, upt_v),
        (up_c, upc_v),
        (coup, cpl_v),
    )
    loads = [pltpu.make_async_copy(s, v, loc_sem.at[i]) for i, (s, v) in enumerate(pairs)]

    @pl.loop(0, LEAVES)
    def _(k):
        own_copy(k).start()

    for load in loads:
        load.start()

    @pl.loop(0, LEAVES)
    def _(k):
        own_copy(k).wait()

    for j in range(6):
        for c in range(4):
            wanted = jnp.maximum(sleaf[j, c, d], 0)
            stage[j, c] = own[wanted]

    @pl.loop(0, LEAVES, unroll=8)
    def _(k):
        buf[k, my_rows, :] = own[k]

    pl.semaphore_wait(barrier, 3 + len(GREET))

    own_sends = [
        pltpu.make_async_remote_copy(
            src_ref=own,
            dst_ref=buf.at[pl.ds(0, LEAVES), my_rows, :],
            send_sem=xs_sem.at[o - 1],
            recv_sem=xr_sem.at[o - 1],
            device_id={"rhs": rhs_at(o)},
            device_id_type=MESH,
        )
        for o in (1, 2, 3)
    ]
    halo_sends = [
        pltpu.make_async_remote_copy(
            src_ref=stage.at[j],
            dst_ref=buf.at[pl.ds(LEAVES + 4 * j, 4), my_rows, :],
            send_sem=hs_sem.at[j],
            recv_sem=hr_sem.at[j],
            device_id={"leaf": leaf_at(FACES[j])},
            device_id_type=MESH,
        )
        for j in range(6)
    ]
    for send in halo_sends:
        send.start()
    for send in own_sends:
        send.start()

    loads[0].wait()

    @pl.loop(0, LEAVES, unroll=4)
    def _(t):
        b = bas_v[:, pl.ds(pl.multiple_of(t * WIDTH, WIDTH), WIDTH)]
        high, low = halves(b)
        b_hi[t] = high
        b_lo[t] = low
        w = jnp.concatenate([high, low], axis=1)
        x = own[t]
        r = dot_nt(jnp.concatenate([x, x], axis=1), jnp.concatenate([w] * 4, axis=0))
        f_rep[t] = r
        x_up[LEAVES + t] = coef_form(r)

    loads[1].wait()
    for a in range(8):
        blk = jnp.concatenate([loc_v[8 * b + a] for b in range(4)], axis=0)
        ef[pl.ds(64 * a, 64), :] = blk.T

    @pl.loop(2, 64, unroll=2)
    def _(n):
        m = unfold(ef[pl.ds(n, 8, stride=64), :])
        high = m.astype(BF16)
        rest = m - high.astype(F32)
        e_hi[n] = high
        e_lo[n] = rest.astype(BF16)
        e_v[n] = jnp.where(lane_group(m.shape) < 2, high.astype(F32), rest).astype(BF16)

    def lift(p):
        x = jnp.concatenate([x_up[2 * p], x_up[2 * p + 1]], axis=1)
        w = jnp.concatenate(
            [
                rows_form(e_hi[2 * p], e_lo[2 * p]),
                rows_form(e_hi[2 * p + 1], e_lo[2 * p + 1]),
            ],
            axis=0,
        )
        x_up[p] = coef_form(dot_nn(x, w))

    for width in (16, 8, 4, 2, 1):

        @pl.loop(width, 2 * width, unroll=min(width, 4))
        def _(p):
            lift(p)

    lvl[0] = x_up[1]

    def level_sends(level):
        step = 2**level
        side = 1 - 2 * lax.rem(lax.div(d, step), 2)
        targets = [
            leaf_at(2 * step),
            leaf_at(-2 * step),
            lax.rem(d + 3 * step * side + 2 * NLEAF, NLEAF),
        ]
        if level < 4:
            targets.append(d + step * side)
        return [
            pltpu.make_async_remote_copy(
                src_ref=lvl.at[level],
                dst_ref=lrecv.at[level, i],
                send_sem=ls_sem.at[level, i],
                recv_sem=lr_sem.at[level, i],
                device_id={"leaf": target},
                device_id_type=MESH,
            )
            for i, target in enumerate(targets)
        ]

    sends = [level_sends(level) for level in range(5)]

    def start_level(level):
        for send in reversed(sends[level]):
            send.start()

    start_level(0)

    for send in halo_sends:
        send.wait_recv()
    halo_fwd = [
        pltpu.make_async_remote_copy(
            src_ref=buf.at[pl.ds(LEAVES, 24), my_rows, :],
            dst_ref=buf.at[pl.ds(LEAVES, 24), my_rows, :],
            send_sem=ys_sem.at[o - 1],
            recv_sem=yr_sem.at[o - 1],
            device_id={"rhs": rhs_at(o)},
            device_id_type=MESH,
        )
        for o in (1, 2, 3)
    ]
    for send in halo_fwd:
        send.start()

    loads[3].wait()
    for a in range(8):
        blk = jnp.concatenate([upt_v[8 * b + a] for b in range(4)], axis=0)
        uf[pl.ds(128 * a, 128), :] = blk.T
    loads[4].wait()
    for c in range(3):
        for a in range(8):
            blk = jnp.concatenate([upc_v[c, 8 * b + a] for b in range(4)], axis=0)
            cf[pl.ds(1024 * c + 128 * a, 128), :] = blk.T

    def node_at(level):
        return lax.div(d + NLEAF, 2**level)

    def lift_level(level):
        n = node_at(level)
        twin = n + 1 - 2 * lax.rem(n, 2)
        x = jnp.concatenate([lvl[level], lrecv[level, 3]], axis=1)
        w = jnp.concatenate(
            [
                rows_form(*halves(unfold(uf[pl.ds(n, 8, stride=128), :]))),
                rows_form(*halves(unfold(uf[pl.ds(twin, 8, stride=128), :]))),
            ],
            axis=0,
        )
        lvl[level + 1] = coef_form(dot_nn(x, w))

    def leaf_coupling(first, count):
        @pl.loop(first, first + count, unroll=2)
        def _(t):
            group = lane_group((COLS, 128))
            x_high, x_low, c_high, c_low = [], [], [], []
            for half in range(2):
                g = [f_rep[fsrc[4 * half + j, t]] for j in range(4)]
                g = jnp.where(
                    group < 2,
                    jnp.where(group == 0, g[0], g[1]),
                    jnp.where(group == 2, g[2], g[3]),
                )
                high, low = halves(g)
                x_high.append(high)
                x_low.append(low)
                m = jnp.concatenate([cpl_v[t, 4 * half + j] for j in range(4)], axis=1)
                high, low = halves(m)
                c_high.append(high)
                c_low.append(low)
            x = jnp.concatenate(x_high + x_low + x_high, axis=1)
            w = jnp.concatenate(c_high + c_high + c_low, axis=1)
            ll[t] = dot_nt(x, jnp.concatenate([w] * 4, axis=0))

    loads[5].wait()
    for level in range(4):
        leaf_coupling(8 * level, 8)
        sends[level][3].wait_recv()
        lift_level(level)
        start_level(level + 1)

    loads[2].wait()
    for send in own_sends + halo_fwd:
        send.wait_recv()
    part_sends = []
    for chunk in range(CHUNKS):

        @pl.loop(chunk * CHUNK, (chunk + 1) * CHUNK, unroll=4)
        def _(t):
            x = jnp.concatenate([buf[nsrc[0, t]], buf[nsrc[1, t]]], axis=1)
            w = jnp.concatenate([blk_v[t, 0], blk_v[t, 1]], axis=1)
            o = dot_nt(x, w)
            for q in range(NRHS):
                part[q, t] = o[COLS * q : COLS * (q + 1)]

        for o in (2, 1, 3):
            piece = pl.ds(chunk * CHUNK, CHUNK)
            send = pltpu.make_async_remote_copy(
                src_ref=part.at[rhs_at(o), piece],
                dst_ref=rbuf.at[o - 1, piece],
                send_sem=rs_sem.at[o - 1, chunk],
                recv_sem=rr_sem.at[o - 1, chunk],
                device_id={"rhs": rhs_at(o)},
                device_id_type=MESH,
            )
            send.start()
            part_sends.append(send)

    field = None
    for level in (4, 3, 2, 1, 0):
        width = NLEAF // 2**level
        n = node_at(level)
        t = n - width
        even = lax.rem(t, 2) == 0
        valid = [t + 2 <= width - 1, t >= 2, jnp.where(even, t + 3 <= width - 1, t >= 3)]
        for send in sends[level][:3]:
            send.wait_recv()
        xs, ws = [], []
        for slot, ok, c in ((0, valid[1], 0), (1, valid[0], 1), (2, valid[2], 2)):
            got = lrecv[level, slot].astype(F32)
            xs.append((got * ok.astype(F32)).astype(BF16))
            ws.append(lanes_form(unfold(cf[pl.ds(1024 * c + n, 8, stride=128), :])))
        if field is not None:
            xs.append(coef_form(field))
            ws.append(lanes_form(unfold(uf[pl.ds(n, 8, stride=128), :])))
        field = dot_nt(jnp.concatenate(xs, axis=1), jnp.concatenate(ws, axis=1))

    x_dn[1] = coef_form(field)
    for width in (2, 4, 8, 16):

        @pl.loop(width, 2 * width, unroll=min(width, 4))
        def _(h):
            r = dot_nt(x_dn[lax.div(h, 2)], jnp.concatenate([e_v[h]] * 4, axis=0))
            x_dn[h] = coef_form(r)

    @pl.loop(0, LEAVES, unroll=4)
    def _(t):
        h = t + LEAVES
        r = dot_nt(x_dn[lax.div(h, 2)], jnp.concatenate([e_v[h]] * 4, axis=0))
        x = coef_form(r + ll[t])
        acc[t] = dot_nn(x, rows_form(b_hi[t], b_lo[t]))

    for chunk in range(CHUNKS):
        for send in part_sends[3 * chunk : 3 * chunk + 3]:
            send.wait_recv()

        @pl.loop(chunk * CHUNK, (chunk + 1) * CHUNK, unroll=4)
        def _(t):
            near = (part[me, t] + rbuf[0, t]) + (rbuf[1, t] + rbuf[2, t])
            out[:, pl.ds(pl.multiple_of(t * WIDTH, WIDTH), WIDTH)] = near + acc[t]

    for send in own_sends + halo_sends + halo_fwd + part_sends:
        send.wait_send()
    for group in sends:
        for send in group:
            send.wait_send()


def local(dens, bases, blocks, near_src, send_leaf, far_src, coupling, local_t, upper_t, up_c):
    any_spec = pl.BlockSpec(memory_space=pl.ANY)
    smem_spec = pl.BlockSpec(memory_space=pltpu.SMEM)
    dma = pltpu.SemaphoreType.DMA
    vmem = pltpu.VMEM
    return pl.pallas_call(
        kernel,
        out_shape=jax.ShapeDtypeStruct((COLS, LEAVES * WIDTH), F32),
        in_specs=[any_spec] * 3 + [smem_spec] * 3 + [any_spec] * 4,
        out_specs=pl.BlockSpec(memory_space=pltpu.VMEM),
        scratch_shapes=[
            vmem((LEAVES, COLS, WIDTH), BF16),
            vmem((SLOTS, NRHS * COLS, WIDTH), BF16),
            vmem((6, 4, COLS, WIDTH), BF16),
            vmem((32, LEAVES * WIDTH), F32),
            vmem((LEAVES, 2, WIDTH, WIDTH), BF16),
            vmem((LEAVES, 8, 32, 32), F32),
            vmem((32, 32, 64), F32),
            vmem((32, 32, 128), F32),
            vmem((3, 32, 32, 128), F32),
            vmem((512, 128), F32),
            vmem((1024, 128), F32),
            vmem((3072, 128), F32),
            vmem((64, 32, 128), BF16),
            vmem((64, 32, 128), BF16),
            vmem((64, 32, 128), BF16),
            vmem((LEAVES, 32, 128), BF16),
            vmem((LEAVES, 32, 128), BF16),
            vmem((LEAVES, COLS, 128), F32),
            vmem((64, COLS, 128), BF16),
            vmem((LEAVES, COLS, 128), BF16),
            vmem((LEAVES, COLS, 128), F32),
            vmem((LEAVES, COLS, 128), F32),
            vmem((5, COLS, 128), BF16),
            vmem((5, 4, COLS, 128), BF16),
            vmem((NRHS, LEAVES, COLS, WIDTH), F32),
            vmem((3, LEAVES, COLS, WIDTH), F32),
            dma((LEAVES,)),
            dma((6,)),
            dma((3,)),
            dma((3,)),
            dma((6,)),
            dma((6,)),
            dma((3,)),
            dma((3,)),
            dma((5, 4)),
            dma((5, 4)),
            dma((3, CHUNKS)),
            dma((3, CHUNKS)),
        ],
        compiler_params=pltpu.CompilerParams(
            collective_id=0, has_side_effects=True, vmem_limit_bytes=48 * 2**20
        ),
        name="h2_product",
    )(
        dens,
        bases,
        blocks,
        near_src.T,
        send_leaf.transpose(1, 2, 0),
        far_src.T,
        coupling,
        local_t[0].transpose(1, 2, 0),
        upper_t.transpose(1, 2, 0),
        up_c.transpose(1, 2, 3, 0),
    )


def solution(mesh):
    in_specs = (
        P("rhs", "leaf"),
        P(None, "leaf"),
        P("leaf", "rhs", None, None),
        P("leaf", "rhs"),
        P(),
        P("leaf", None),
        P("leaf", None, None, None),
        P("leaf", None, None, None),
        P(),
        P(),
    )
    return jax.shard_map(
        local, mesh=mesh, in_specs=in_specs, out_specs=P("rhs", "leaf"), check_vma=False
    )
```

```python
import functools

import jax
import jax.numpy as jnp
from jax import lax
from jax.experimental import pallas as pl
from jax.experimental.pallas import tpu as pltpu
from jax.sharding import PartitionSpec as P

F32 = jnp.float32
BF16 = jnp.bfloat16
MESH = pl.DeviceIdType.MESH
LEAVES = 32
WIDTH = 128
COLS = 16
NLEAF = 64
NRHS = 4
SLOTS = 56
FACES = (1, -1, 4, -4, 16, -16)
GREET = (1, -1, 2, -2, 3, -3, 4, -4, 6, -6, 8, -8, 12, -12, 16, -16, 24, -24, 32)
CHUNKS = 4
CHUNK = LEAVES // CHUNKS


def dot_nn(a, b):
    return lax.dot_general(a, b, (((1,), (0,)), ((), ())), preferred_element_type=F32)


def dot_nt(a, b):
    return lax.dot_general(a, b, (((1,), (1,)), ((), ())), preferred_element_type=F32)


def halves(x):
    high = x.astype(BF16)
    return high, (x - high.astype(F32)).astype(BF16)


def lane_group(shape):
    return lax.broadcasted_iota(jnp.int32, shape, len(shape) - 1) // 32


def coef_form(r):
    group = lane_group(r.shape)
    high = r.astype(BF16).astype(F32)
    return jnp.where(group % 2 == 0, high, r - high).astype(BF16)


def unfold(tile):
    group = lane_group(tile.shape)
    turned = [tile] + [pltpu.roll(tile, 32 * k, 1) for k in (1, 2, 3)]
    rows = []
    for b in range(4):
        pick = [turned[(g - b) % 4] for g in range(4)]
        rows.append(
            jnp.where(
                group < 2,
                jnp.where(group == 0, pick[0], pick[1]),
                jnp.where(group == 2, pick[2], pick[3]),
            )
        )
    return jnp.concatenate(rows, axis=0)


def rows_form(high, low):
    return jnp.concatenate([high, high, low, low], axis=0)


def lanes_form(m):
    high = m.astype(BF16).astype(F32)
    v = jnp.where(lane_group(m.shape) < 2, high, m - high).astype(BF16)
    return jnp.concatenate([v] * 4, axis=0)


def kernel(
    dens,
    bases,
    blocks,
    nsrc_h,
    sleaf_h,
    fsrc_h,
    coup,
    loc_t,
    up_t,
    up_c,
    out,
    nsrc,
    sleaf,
    fsrc,
    own,
    buf,
    stage,
    bas_v,
    blk_v,
    cpl_v,
    loc_v,
    upt_v,
    upc_v,
    ef,
    uf,
    cf,
    e_hi,
    e_lo,
    e_v,
    b_hi,
    b_lo,
    f_rep,
    x_up,
    x_dn,
    ll,
    acc,
    lvl,
    lrecv,
    part,
    rbuf,
    own_sem,
    loc_sem,
    xs_sem,
    xr_sem,
    hs_sem,
    hr_sem,
    ys_sem,
    yr_sem,
    ls_sem,
    lr_sem,
    rs_sem,
    rr_sem,
):
    d = lax.axis_index("leaf")
    me = lax.axis_index("rhs")
    my_rows = pl.ds(pl.multiple_of(me * COLS, COLS), COLS)

    def leaf_at(offset):
        return lax.rem(d + (offset + 2 * NLEAF), NLEAF)

    def rhs_at(offset):
        return lax.rem(me + offset, NRHS)

    barrier = pltpu.get_barrier_semaphore()
    for offset in (1, 2, 3):
        pl.semaphore_signal(barrier, inc=1, device_id={"rhs": rhs_at(offset)}, device_id_type=MESH)
    for offset in GREET:
        pl.semaphore_signal(
            barrier, inc=1, device_id={"leaf": leaf_at(offset)}, device_id_type=MESH
        )

    def own_copy(k):
        return pltpu.make_async_copy(
            dens.at[:, pl.ds(pl.multiple_of(k * WIDTH, WIDTH), WIDTH)], own.at[k], own_sem.at[k]
        )

    pairs = (
        (bases, bas_v),
        (loc_t, loc_v),
        (blocks, blk_v),
        (up_t, upt_v),
        (up_c, upc_v),
        (coup, cpl_v),
        (nsrc_h, nsrc),
        (sleaf_h, sleaf),
        (fsrc_h, fsrc),
    )
    loads = [pltpu.make_async_copy(s, v, loc_sem.at[i]) for i, (s, v) in enumerate(pairs)]

    @pl.loop(0, LEAVES)
    def _(k):
        own_copy(k).start()

    loads[7].start()
    for load in loads[:7] + loads[8:]:
        load.start()

    @pl.loop(0, LEAVES)
    def _(k):
        own_copy(k).wait()

    loads[7].wait()

    for j in range(6):
        for c in range(4):
            wanted = jnp.maximum(sleaf[j, c, d], 0)
            stage[j, c] = own[wanted]

    @pl.loop(0, LEAVES, unroll=8)
    def _(k):
        buf[k, my_rows, :] = own[k]

    pl.semaphore_wait(barrier, 3 + len(GREET))

    own_sends = [
        pltpu.make_async_remote_copy(
            src_ref=own,
            dst_ref=buf.at[pl.ds(0, LEAVES), my_rows, :],
            send_sem=xs_sem.at[o - 1],
            recv_sem=xr_sem.at[o - 1],
            device_id={"rhs": rhs_at(o)},
            device_id_type=MESH,
        )
        for o in (1, 2, 3)
    ]
    halo_sends = [
        pltpu.make_async_remote_copy(
            src_ref=stage.at[j],
            dst_ref=buf.at[pl.ds(LEAVES + 4 * j, 4), my_rows, :],
            send_sem=hs_sem.at[j],
            recv_sem=hr_sem.at[j],
            device_id={"leaf": leaf_at(FACES[j])},
            device_id_type=MESH,
        )
        for j in range(6)
    ]
    for send in halo_sends:
        send.start()
    for send in own_sends:
        send.start()

    loads[0].wait()

    @pl.loop(0, LEAVES, unroll=4)
    def _(t):
        b = bas_v[:, pl.ds(pl.multiple_of(t * WIDTH, WIDTH), WIDTH)]
        high, low = halves(b)
        b_hi[t] = high
        b_lo[t] = low
        w = jnp.concatenate([high, low], axis=1)
        x = own[t]
        r = dot_nt(jnp.concatenate([x, x], axis=1), jnp.concatenate([w] * 4, axis=0))
        f_rep[t] = r
        x_up[LEAVES + t] = coef_form(r)

    loads[1].wait()
    for a in range(8):
        blk = jnp.concatenate([loc_v[8 * b + a] for b in range(4)], axis=0)
        ef[pl.ds(64 * a, 64), :] = blk.T

    @pl.loop(2, 64, unroll=2)
    def _(n):
        m = unfold(ef[pl.ds(n, 8, stride=64), :])
        high = m.astype(BF16)
        rest = m - high.astype(F32)
        e_hi[n] = high
        e_lo[n] = rest.astype(BF16)
        e_v[n] = jnp.where(lane_group(m.shape) < 2, high.astype(F32), rest).astype(BF16)

    def lift(p):
        x = jnp.concatenate([x_up[2 * p], x_up[2 * p + 1]], axis=1)
        w = jnp.concatenate(
            [
                rows_form(e_hi[2 * p], e_lo[2 * p]),
                rows_form(e_hi[2 * p + 1], e_lo[2 * p + 1]),
            ],
            axis=0,
        )
        x_up[p] = coef_form(dot_nn(x, w))

    for width in (16, 8, 4, 2, 1):

        @pl.loop(width, 2 * width, unroll=min(width, 4))
        def _(p):
            lift(p)

    lvl[0] = x_up[1]

    def level_sends(level):
        step = 2**level
        side = 1 - 2 * lax.rem(lax.div(d, step), 2)
        targets = [
            leaf_at(2 * step),
            leaf_at(-2 * step),
            lax.rem(d + 3 * step * side + 2 * NLEAF, NLEAF),
        ]
        if level < 4:
            targets.append(d + step * side)
        return [
            pltpu.make_async_remote_copy(
                src_ref=lvl.at[level],
                dst_ref=lrecv.at[level, i],
                send_sem=ls_sem.at[level, i],
                recv_sem=lr_sem.at[level, i],
                device_id={"leaf": target},
                device_id_type=MESH,
            )
            for i, target in enumerate(targets)
        ]

    sends = [level_sends(level) for level in range(5)]

    def start_level(level):
        for send in reversed(sends[level]):
            send.start()

    start_level(0)

    for send in halo_sends:
        send.wait_recv()
    halo_fwd = [
        pltpu.make_async_remote_copy(
            src_ref=buf.at[pl.ds(LEAVES, 24), my_rows, :],
            dst_ref=buf.at[pl.ds(LEAVES, 24), my_rows, :],
            send_sem=ys_sem.at[o - 1],
            recv_sem=yr_sem.at[o - 1],
            device_id={"rhs": rhs_at(o)},
            device_id_type=MESH,
        )
        for o in (1, 2, 3)
    ]
    for send in halo_fwd:
        send.start()

    loads[3].wait()
    for a in range(8):
        blk = jnp.concatenate([upt_v[8 * b + a] for b in range(4)], axis=0)
        uf[pl.ds(128 * a, 128), :] = blk.T
    loads[4].wait()
    for c in range(3):
        for a in range(8):
            blk = jnp.concatenate([upc_v[c, 8 * b + a] for b in range(4)], axis=0)
            cf[pl.ds(1024 * c + 128 * a, 128), :] = blk.T

    def node_at(level):
        return lax.div(d + NLEAF, 2**level)

    def lift_level(level):
        n = node_at(level)
        twin = n + 1 - 2 * lax.rem(n, 2)
        x = jnp.concatenate([lvl[level], lrecv[level, 3]], axis=1)
        w = jnp.concatenate(
            [
                rows_form(*halves(unfold(uf[pl.ds(n, 8, stride=128), :]))),
                rows_form(*halves(unfold(uf[pl.ds(twin, 8, stride=128), :]))),
            ],
            axis=0,
        )
        lvl[level + 1] = coef_form(dot_nn(x, w))

    def leaf_coupling(first, count):
        @pl.loop(first, first + count, unroll=2)
        def _(t):
            group = lane_group((COLS, 128))
            x_high, x_low, c_high, c_low = [], [], [], []
            for half in range(2):
                g = [f_rep[fsrc[4 * half + j, t]] for j in range(4)]
                g = jnp.where(
                    group < 2,
                    jnp.where(group == 0, g[0], g[1]),
                    jnp.where(group == 2, g[2], g[3]),
                )
                high, low = halves(g)
                x_high.append(high)
                x_low.append(low)
                m = jnp.concatenate([cpl_v[t, 4 * half + j] for j in range(4)], axis=1)
                high, low = halves(m)
                c_high.append(high)
                c_low.append(low)
            x = jnp.concatenate(x_high + x_low + x_high, axis=1)
            w = jnp.concatenate(c_high + c_high + c_low, axis=1)
            ll[t] = dot_nt(x, jnp.concatenate([w] * 4, axis=0))

    loads[5].wait()
    loads[8].wait()
    for level in range(4):
        leaf_coupling(8 * level, 8)
        sends[level][3].wait_recv()
        lift_level(level)
        start_level(level + 1)

    loads[2].wait()
    loads[6].wait()
    for send in own_sends + halo_fwd:
        send.wait_recv()
    part_sends = []
    for chunk in range(CHUNKS):

        @pl.loop(chunk * CHUNK, (chunk + 1) * CHUNK, unroll=4)
        def _(t):
            x = jnp.concatenate([buf[nsrc[0, t]], buf[nsrc[1, t]]], axis=1)
            w = jnp.concatenate([blk_v[t, 0], blk_v[t, 1]], axis=1)
            o = dot_nt(x, w)
            for q in range(NRHS):
                part[q, t] = o[COLS * q : COLS * (q + 1)]

        for o in (2, 1, 3):
            piece = pl.ds(chunk * CHUNK, CHUNK)
            send = pltpu.make_async_remote_copy(
                src_ref=part.at[rhs_at(o), piece],
                dst_ref=rbuf.at[o - 1, piece],
                send_sem=rs_sem.at[o - 1, chunk],
                recv_sem=rr_sem.at[o - 1, chunk],
                device_id={"rhs": rhs_at(o)},
                device_id_type=MESH,
            )
            send.start()
            part_sends.append(send)

    field = None
    for level in (4, 3, 2, 1, 0):
        width = NLEAF // 2**level
        n = node_at(level)
        t = n - width
        even = lax.rem(t, 2) == 0
        valid = [t + 2 <= width - 1, t >= 2, jnp.where(even, t + 3 <= width - 1, t >= 3)]
        for send in sends[level][:3]:
            send.wait_recv()
        xs, ws = [], []
        for slot, ok, c in ((0, valid[1], 0), (1, valid[0], 1), (2, valid[2], 2)):
            got = lrecv[level, slot].astype(F32)
            xs.append((got * ok.astype(F32)).astype(BF16))
            ws.append(lanes_form(unfold(cf[pl.ds(1024 * c + n, 8, stride=128), :])))
        if field is not None:
            xs.append(coef_form(field))
            ws.append(lanes_form(unfold(uf[pl.ds(n, 8, stride=128), :])))
        field = dot_nt(jnp.concatenate(xs, axis=1), jnp.concatenate(ws, axis=1))

    x_dn[1] = coef_form(field)
    for width in (2, 4, 8, 16):

        @pl.loop(width, 2 * width, unroll=min(width, 4))
        def _(h):
            r = dot_nt(x_dn[lax.div(h, 2)], jnp.concatenate([e_v[h]] * 4, axis=0))
            x_dn[h] = coef_form(r)

    @pl.loop(0, LEAVES, unroll=4)
    def _(t):
        h = t + LEAVES
        r = dot_nt(x_dn[lax.div(h, 2)], jnp.concatenate([e_v[h]] * 4, axis=0))
        x = coef_form(r + ll[t])
        acc[t] = dot_nn(x, rows_form(b_hi[t], b_lo[t]))

    for chunk in range(CHUNKS):
        for send in part_sends[3 * chunk : 3 * chunk + 3]:
            send.wait_recv()

        @pl.loop(chunk * CHUNK, (chunk + 1) * CHUNK, unroll=4)
        def _(t):
            near = (part[me, t] + rbuf[0, t]) + (rbuf[1, t] + rbuf[2, t])
            out[:, pl.ds(pl.multiple_of(t * WIDTH, WIDTH), WIDTH)] = near + acc[t]

    for send in own_sends + halo_sends + halo_fwd + part_sends:
        send.wait_send()
    for group in sends:
        for send in group:
            send.wait_send()


def local(dens, bases, blocks, near_src, send_leaf, far_src, coupling, local_t, upper_t, up_c):
    any_spec = pl.BlockSpec(memory_space=pltpu.HBM)
    dma = pltpu.SemaphoreType.DMA
    vmem = pltpu.VMEM
    return pl.pallas_call(
        kernel,
        out_shape=jax.ShapeDtypeStruct((COLS, LEAVES * WIDTH), F32),
        in_specs=[any_spec] * 10,
        out_specs=pl.BlockSpec(memory_space=pltpu.VMEM),
        scratch_shapes=[
            pltpu.SMEM((2, LEAVES), jnp.int32),
            pltpu.SMEM((6, 4, NLEAF), jnp.int32),
            pltpu.SMEM((8, LEAVES), jnp.int32),
            vmem((LEAVES, COLS, WIDTH), BF16),
            vmem((SLOTS, NRHS * COLS, WIDTH), BF16),
            vmem((6, 4, COLS, WIDTH), BF16),
            vmem((32, LEAVES * WIDTH), F32),
            vmem((LEAVES, 2, WIDTH, WIDTH), BF16),
            vmem((LEAVES, 8, 32, 32), F32),
            vmem((32, 32, 64), F32),
            vmem((32, 32, 128), F32),
            vmem((3, 32, 32, 128), F32),
            vmem((512, 128), F32),
            vmem((1024, 128), F32),
            vmem((3072, 128), F32),
            vmem((64, 32, 128), BF16),
            vmem((64, 32, 128), BF16),
            vmem((64, 32, 128), BF16),
            vmem((LEAVES, 32, 128), BF16),
            vmem((LEAVES, 32, 128), BF16),
            vmem((LEAVES, COLS, 128), F32),
            vmem((64, COLS, 128), BF16),
            vmem((LEAVES, COLS, 128), BF16),
            vmem((LEAVES, COLS, 128), F32),
            vmem((LEAVES, COLS, 128), F32),
            vmem((5, COLS, 128), BF16),
            vmem((5, 4, COLS, 128), BF16),
            vmem((NRHS, LEAVES, COLS, WIDTH), F32),
            vmem((3, LEAVES, COLS, WIDTH), F32),
            dma((LEAVES,)),
            dma((9,)),
            dma((3,)),
            dma((3,)),
            dma((6,)),
            dma((6,)),
            dma((3,)),
            dma((3,)),
            dma((5, 4)),
            dma((5, 4)),
            dma((3, CHUNKS)),
            dma((3, CHUNKS)),
        ],
        compiler_params=pltpu.CompilerParams(
            collective_id=0, has_side_effects=True, vmem_limit_bytes=60 * 2**20
        ),
        name="h2_product",
    )(
        dens,
        bases,
        blocks,
        near_src.T,
        send_leaf.transpose(1, 2, 0),
        far_src.T,
        coupling,
        local_t[0].transpose(1, 2, 0),
        upper_t.transpose(1, 2, 0),
        up_c.transpose(1, 2, 3, 0),
    )


def solution(mesh):
    in_specs = (
        P("rhs", "leaf"),
        P(None, "leaf"),
        P("leaf", "rhs", None, None),
        P("leaf", "rhs"),
        P(),
        P("leaf", None),
        P("leaf", None, None, None),
        P("leaf", None, None, None),
        P(),
        P(),
    )
    return jax.shard_map(
        local, mesh=mesh, in_specs=in_specs, out_specs=P("rhs", "leaf"), check_vma=False
    )
```

```python
import functools

import jax
import jax.numpy as jnp
from jax import lax
from jax.experimental import pallas as pl
from jax.experimental.pallas import tpu as pltpu
from jax.sharding import PartitionSpec as P

F32 = jnp.float32
BF16 = jnp.bfloat16
MESH = pl.DeviceIdType.MESH
LEAVES = 32
WIDTH = 128
COLS = 16
NLEAF = 64
NRHS = 4
SLOTS = 56
FACES = (1, -1, 4, -4, 16, -16)
GREET = (1, -1, 3, -3) + tuple(range(2, 64, 2))


def dot_nn(a, b):
    return lax.dot_general(a, b, (((1,), (0,)), ((), ())), preferred_element_type=F32)


def dot_nt(a, b):
    return lax.dot_general(a, b, (((1,), (1,)), ((), ())), preferred_element_type=F32)


def halves(x):
    high = x.astype(BF16)
    return high, (x - high.astype(F32)).astype(BF16)


def lane_group(shape):
    return lax.broadcasted_iota(jnp.int32, shape, len(shape) - 1) // 32


def coef_form(r):
    group = lane_group(r.shape)
    high = r.astype(BF16).astype(F32)
    return jnp.where(group % 2 == 0, high, r - high).astype(BF16)


def unfold(tile):
    group = lane_group(tile.shape)
    turned = [tile] + [pltpu.roll(tile, 32 * k, 1) for k in (1, 2, 3)]
    rows = []
    for b in range(4):
        pick = [turned[(g - b) % 4] for g in range(4)]
        rows.append(
            jnp.where(
                group < 2,
                jnp.where(group == 0, pick[0], pick[1]),
                jnp.where(group == 2, pick[2], pick[3]),
            )
        )
    return jnp.concatenate(rows, axis=0)


def rows_form(high, low):
    return jnp.concatenate([high, high, low, low], axis=0)


def lanes_form(m):
    high = m.astype(BF16).astype(F32)
    v = jnp.where(lane_group(m.shape) < 2, high, m - high).astype(BF16)
    return jnp.concatenate([v] * 4, axis=0)


def kernel(
    dens,
    bases,
    blocks,
    nsrc_h,
    sleaf_h,
    fsrc_h,
    coup,
    loc_t,
    up_t,
    up_c,
    out,
    nsrc,
    sleaf,
    fsrc,
    own,
    buf,
    stage,
    bas_v,
    blk_v,
    cpl_v,
    loc_v,
    upt_v,
    upc_v,
    ef,
    uf,
    cf,
    e_v,
    b_hi,
    b_lo,
    q_hi,
    q_lo,
    t_x,
    f_rep,
    acc,
    m_rep,
    m_hi,
    m_lo,
    root_x,
    pair_x,
    lrecv,
    chips,
    part,
    raw,
    rbuf,
    own_sem,
    loc_sem,
    os_sem,
    or_sem,
    hs_sem,
    hr_sem,
    ys_sem,
    yr_sem,
    ls_sem,
    lr_sem,
    gs_sem,
    gr_sem,
    ps_sem,
    pr_sem,
):
    d = lax.axis_index("leaf")
    me = lax.axis_index("rhs")

    def leaf_at(offset):
        return lax.rem(d + (offset + 2 * NLEAF), NLEAF)

    def rhs_at(offset):
        return lax.rem(me + offset, NRHS)

    right, across, left = rhs_at(1), rhs_at(2), rhs_at(3)

    def rows_of(r):
        return pl.ds(pl.multiple_of(r * COLS, COLS), COLS)

    my_rows = rows_of(me)

    barrier = pltpu.get_barrier_semaphore()
    for peer in (right, left):
        pl.semaphore_signal(barrier, inc=1, device_id={"rhs": peer}, device_id_type=MESH)
    for offset in GREET:
        pl.semaphore_signal(
            barrier, inc=1, device_id={"leaf": leaf_at(offset)}, device_id_type=MESH
        )

    def own_copy(k):
        return pltpu.make_async_copy(
            dens.at[:, pl.ds(pl.multiple_of(k * WIDTH, WIDTH), WIDTH)], own.at[k], own_sem.at[k]
        )

    pairs = (
        (loc_t, loc_v),
        (bases, bas_v),
        (sleaf_h, sleaf),
        (up_t, upt_v),
        (coup, cpl_v),
        (fsrc_h, fsrc),
        (blocks, blk_v),
        (nsrc_h, nsrc),
        (up_c, upc_v),
    )
    loads = [pltpu.make_async_copy(s, v, loc_sem.at[i]) for i, (s, v) in enumerate(pairs)]
    for load in loads[:3]:
        load.start()

    @pl.loop(0, LEAVES)
    def _(k):
        own_copy(k).start()

    for load in loads[3:]:
        load.start()

    loads[0].wait()
    for a in range(8):
        blk = jnp.concatenate([loc_v[pl.ds(32 * (8 * b + a), 32), :] for b in range(4)], axis=0)
        ef[pl.ds(64 * a, 64), :] = blk.T

    @pl.loop(0, 64, unroll=8)
    def _(n):
        m = unfold(ef[pl.ds(n, 8, stride=64), :])
        high = m.astype(BF16).astype(F32)
        e_v[n] = jnp.where(lane_group(m.shape) < 2, high, m - high).astype(BF16)

    row = lax.broadcasted_iota(jnp.int32, (32, 128), 0)
    lane = lax.broadcasted_iota(jnp.int32, (32, 128), 1)
    t_x[1] = jnp.where((lane % 64) == row, 1.0, 0.0).astype(BF16)
    for width in (2, 4, 8, 16, 32):
        for p in range(width // 2, width):
            w = jnp.concatenate([e_v[2 * p], e_v[2 * p + 1]], axis=0)
            r = dot_nt(t_x[p], w)
            t_x[2 * p] = coef_form(jnp.concatenate([r[:, :32]] * 4, axis=1))
            t_x[2 * p + 1] = coef_form(jnp.concatenate([r[:, 32:]] * 4, axis=1))

    loads[1].wait()

    @pl.loop(0, LEAVES, unroll=8)
    def _(t):
        high, low = halves(bas_v[:, pl.ds(pl.multiple_of(t * WIDTH, WIDTH), WIDTH)])
        b_hi[t] = high
        b_lo[t] = low
        high, low = halves(dot_nn(t_x[LEAVES + t], rows_form(high, low)))
        q_hi[t] = high
        q_lo[t] = low

    @pl.loop(0, LEAVES)
    def _(k):
        own_copy(k).wait()

    root = jnp.zeros((COLS, 32), F32)
    for t in range(LEAVES):
        x = own[t]
        root = root + dot_nt(
            jnp.concatenate([x, x], axis=1), jnp.concatenate([q_hi[t], q_lo[t]], axis=1)
        )
    root_x[...] = coef_form(jnp.concatenate([root] * 4, axis=1))

    loads[2].wait()
    for j in range(6):
        for c in range(4):
            wanted = jnp.maximum(sleaf[j, c, d], 0)
            stage[j, c] = own[wanted]

    @pl.loop(0, LEAVES, unroll=8)
    def _(k):
        buf[k, my_rows, :] = own[k]

    pl.semaphore_wait(barrier, 2 + len(GREET))

    side = 1 - 2 * lax.rem(d, 2)
    partners = (leaf_at(2), leaf_at(-2), lax.rem(d + 3 * side + NLEAF, NLEAF), d + side)
    root_sends = [
        pltpu.make_async_remote_copy(
            src_ref=root_x,
            dst_ref=lrecv.at[i],
            send_sem=ls_sem.at[i],
            recv_sem=lr_sem.at[i],
            device_id={"leaf": partner},
            device_id_type=MESH,
        )
        for i, partner in enumerate(partners)
    ]
    halo_sends = [
        pltpu.make_async_remote_copy(
            src_ref=stage.at[j],
            dst_ref=buf.at[pl.ds(LEAVES + 4 * j, 4), my_rows, :],
            send_sem=hs_sem.at[j],
            recv_sem=hr_sem.at[j],
            device_id={"leaf": leaf_at(FACES[j])},
            device_id_type=MESH,
        )
        for j in range(6)
    ]

    def over_rhs(src, dst, target, ssem, rsem):
        return pltpu.make_async_remote_copy(
            src_ref=src,
            dst_ref=dst,
            send_sem=ssem,
            recv_sem=rsem,
            device_id={"rhs": target},
            device_id_type=MESH,
        )

    def pass_on(slots, target, source, index, ssem, rsem):
        piece = buf.at[slots, rows_of(source), :]
        return over_rhs(piece, piece, target, ssem.at[index], rsem.at[index])

    lower, upper = pl.ds(0, 16), pl.ds(16, 16)
    own_out = [
        over_rhs(own.at[lower], buf.at[lower, my_rows, :], right, os_sem.at[0], or_sem.at[0]),
        over_rhs(own.at[upper], buf.at[upper, my_rows, :], left, os_sem.at[1], or_sem.at[1]),
        over_rhs(own.at[upper], buf.at[upper, my_rows, :], right, os_sem.at[2], or_sem.at[2]),
        over_rhs(own.at[lower], buf.at[lower, my_rows, :], left, os_sem.at[3], or_sem.at[3]),
    ]
    own_relay = [
        pass_on(lower, right, left, 4, os_sem, or_sem),
        pass_on(upper, left, right, 5, os_sem, or_sem),
    ]
    first, second = pl.ds(LEAVES, 12), pl.ds(LEAVES + 12, 12)
    halo_out = [
        pass_on(first, right, me, 0, ys_sem, yr_sem),
        pass_on(second, left, me, 1, ys_sem, yr_sem),
        pass_on(second, right, me, 2, ys_sem, yr_sem),
        pass_on(first, left, me, 3, ys_sem, yr_sem),
    ]
    halo_relay = [
        pass_on(first, right, left, 4, ys_sem, yr_sem),
        pass_on(second, left, right, 5, ys_sem, yr_sem),
    ]
    root_sends[3].start()
    for send in own_out + halo_sends + root_sends[:3]:
        send.start()

    @pl.loop(0, LEAVES, unroll=8)
    def _(t):
        w = jnp.concatenate([b_hi[t], b_lo[t]], axis=1)
        x = own[t]
        r = dot_nt(jnp.concatenate([x, x], axis=1), w)
        f_rep[t] = jnp.concatenate([r] * 4, axis=1)

    loads[3].wait()
    for a in range(8):
        blk = jnp.concatenate([upt_v[pl.ds(32 * (8 * b + a), 32), :] for b in range(4)], axis=0)
        uf[pl.ds(128 * a, 128), :] = blk.T

    def above(n):
        return unfold(uf[pl.ds(n, 8, stride=128), :])

    n0 = d + NLEAF
    chip = lax.div(d, 2)

    def leaf_coupling(begin, count):
        @pl.loop(begin, begin + count, unroll=4)
        def _(t):
            group = lane_group((COLS, 128))
            x_high, x_low, c_high, c_low = [], [], [], []
            for half in range(2):
                g = [f_rep[fsrc[4 * half + j, t]] for j in range(4)]
                g = jnp.where(
                    group < 2,
                    jnp.where(group == 0, g[0], g[1]),
                    jnp.where(group == 2, g[2], g[3]),
                )
                high, low = halves(g)
                x_high.append(high)
                x_low.append(low)
                m = jnp.concatenate([cpl_v[t, 4 * half + j] for j in range(4)], axis=1)
                high, low = halves(m)
                c_high.append(high)
                c_low.append(low)
            x = jnp.concatenate(x_high + x_low + x_high, axis=1)
            w = jnp.concatenate(c_high + c_high + c_low, axis=1)
            r = dot_nt(x, w)
            x = coef_form(jnp.concatenate([r] * 4, axis=1))
            acc[t] = dot_nn(x, rows_form(b_hi[t], b_lo[t]))

    root_sends[3].wait_recv()
    x = jnp.concatenate([root_x[...], lrecv[3]], axis=1)
    w = jnp.concatenate(
        [rows_form(*halves(above(n0))), rows_form(*halves(above(n0 + side)))], axis=0
    )
    pair = coef_form(dot_nn(x, w))
    pair_x[...] = pair
    chips[chip] = pair
    chip_sends = [
        pltpu.make_async_remote_copy(
            src_ref=pair_x,
            dst_ref=chips.at[chip],
            send_sem=gs_sem.at[k - 1],
            recv_sem=gr_sem.at[k - 1],
            device_id={"leaf": leaf_at(2 * k)},
            device_id_type=MESH,
        )
        for k in range(1, 32)
    ]
    for send in chip_sends:
        send.start()

    loads[4].wait()
    loads[5].wait()
    leaf_coupling(0, 8)

    for send in own_out[:2]:
        send.wait_recv()
    for send in own_relay:
        send.start()
    for send in halo_sends:
        send.wait_recv()
    for send in halo_out:
        send.start()

    leaf_coupling(8, 16)

    for send in halo_out[:2]:
        send.wait_recv()
    for send in halo_relay:
        send.start()

    leaf_coupling(24, 8)

    loads[6].wait()
    loads[7].wait()
    for send in own_out[2:] + own_relay + halo_out[2:] + halo_relay:
        send.wait_recv()

    def near(begin, count):
        @pl.loop(begin, begin + count, unroll=8)
        def _(t):
            x = jnp.concatenate([buf[nsrc[0, t]], buf[nsrc[1, t]]], axis=1)
            w = jnp.concatenate([blk_v[t, 0], blk_v[t, 1]], axis=1)
            o = dot_nt(x, w)
            for q in range(NRHS):
                part[q, t] = o[COLS * q : COLS * (q + 1)]

    def partial(index, dest, t0, count, target, landing):
        return over_rhs(
            part.at[dest, pl.ds(t0, count)], landing, target, ps_sem.at[index], pr_sem.at[index]
        )

    raw_sends = [
        partial(0, across, 0, 8, right, raw.at[0, pl.ds(0, 8)]),
        partial(1, across, 16, 8, left, raw.at[1, pl.ds(0, 8)]),
        partial(2, across, 8, 8, right, raw.at[0, pl.ds(8, 8)]),
        partial(3, across, 24, 8, left, raw.at[1, pl.ds(8, 8)]),
    ]
    plain_sends = [
        partial(4, right, 16, 16, right, rbuf.at[0, upper]),
        partial(5, left, 0, 16, left, rbuf.at[1, lower]),
    ]
    sum_sends = [
        partial(6, right, 0, 8, right, rbuf.at[0, pl.ds(0, 8)]),
        partial(7, left, 16, 8, left, rbuf.at[1, pl.ds(16, 8)]),
        partial(8, right, 8, 8, right, rbuf.at[0, pl.ds(8, 8)]),
        partial(9, left, 24, 8, left, rbuf.at[1, pl.ds(24, 8)]),
    ]
    for i, begin in enumerate((0, 16, 8, 24)):
        near(begin, 8)
        raw_sends[i].start()
    for send in plain_sends:
        send.start()

    def join(i):
        side_of, begin = ((0, 0), (1, 16), (0, 8), (1, 24))[i]
        dest = left if side_of else right
        raw_sends[i].wait_recv()

        @pl.loop(0, 8, unroll=8)
        def _(k):
            t = begin + k
            part[dest, t] = part[dest, t] + raw[side_of, t - 16 * side_of]

        sum_sends[i].start()

    loads[8].wait()
    for c in range(3):
        for a in range(8):
            blk = jnp.concatenate(
                [upc_v[c, pl.ds(8 * b + a, 32, stride=32), :] for b in range(4)], axis=0
            )
            cf[pl.ds(1024 * c + 128 * a, 128), :] = blk.T

    join(0)
    join(1)

    down = None
    couplings = {}
    for level in range(5):
        n = lax.div(n0, 2**level)
        width = NLEAF // 2**level
        t = n - width
        even = lax.rem(t, 2) == 0
        valid = (t >= 2, t + 2 < width, jnp.where(even, t + 3 < width, t >= 3))
        where_to = (n - 2, n + 2, n + 3 - 6 * lax.rem(t, 2))
        cts = []
        for c in range(3):
            ct = unfold(cf[pl.ds(1024 * c + n, 8, stride=128), :])
            cts.append(ct * valid[c].astype(F32))
        if level:
            left_side = jnp.concatenate([coef_form(ct) for ct in cts], axis=0)
            r = dot_nt(left_side, lanes_form(down))
            cts = [r[32 * c : 32 * (c + 1)] for c in range(3)]
        couplings[level] = [
            (jnp.where(ok, place, n), ct) for ok, place, ct in zip(valid, where_to, cts)
        ]
        if level == 0:
            down = above(n0)
        elif level < 4:
            down = dot_nn(coef_form(down), rows_form(*halves(above(n))))

    join(2)
    join(3)

    for n in range(4, 8):
        m_rep[n] = jnp.zeros((32, 128), F32)
    for level in (4, 3, 2, 1):
        width = NLEAF // 2**level
        if level < 4:
            for p in range(width // 2, width):
                lhs = jnp.concatenate(
                    [coef_form(above(2 * p)), coef_form(above(2 * p + 1))], axis=0
                )
                r = dot_nn(lhs, rows_form(*halves(m_rep[p])))
                m_rep[2 * p] = r[:32]
                m_rep[2 * p + 1] = r[32:]
        for place, ct in couplings[level]:
            m_rep[place] = m_rep[place] + ct

    @pl.loop(0, 32, unroll=4)
    def _(e):
        high, low = halves(m_rep[32 + e])
        m_hi[e] = high
        m_lo[e] = low

    for send in root_sends[:3]:
        send.wait_recv()
    field = jnp.zeros((COLS, 128), F32)
    for c in range(3):
        field = field + dot_nn(lrecv[c], rows_form(*halves(couplings[0][c][1])))
    for send in chip_sends:
        send.wait_recv()
    for e in range(0, 32, 2):
        x = jnp.concatenate([chips[e], chips[e + 1]], axis=1)
        w = jnp.concatenate(
            [rows_form(m_hi[e], m_lo[e]), rows_form(m_hi[e + 1], m_lo[e + 1])], axis=0
        )
        field = field + dot_nn(x, w)
    field_x = coef_form(field)

    def finish(begin, count):
        @pl.loop(begin, begin + count, unroll=8)
        def _(t):
            far = acc[t] + dot_nn(field_x, rows_form(q_hi[t], q_lo[t]))
            near_sum = part[me, t] + (rbuf[0, t] + rbuf[1, t])
            out[:, pl.ds(pl.multiple_of(t * WIDTH, WIDTH), WIDTH)] = near_sum + far

    for send in plain_sends + sum_sends:
        send.wait_recv()
    finish(0, LEAVES)

    for send in root_sends + halo_sends + own_out + own_relay + halo_out + halo_relay:
        send.wait_send()
    for send in chip_sends + raw_sends + plain_sends + sum_sends:
        send.wait_send()


def local(dens, bases, blocks, near_src, send_leaf, far_src, coupling, local_t, upper_t, up_c):
    any_spec = pl.BlockSpec(memory_space=pltpu.HBM)
    dma = pltpu.SemaphoreType.DMA
    vmem = pltpu.VMEM
    return pl.pallas_call(
        kernel,
        out_shape=jax.ShapeDtypeStruct((COLS, LEAVES * WIDTH), F32),
        in_specs=[any_spec] * 10,
        out_specs=pl.BlockSpec(memory_space=pltpu.VMEM),
        scratch_shapes=[
            pltpu.SMEM((2, LEAVES), jnp.int32),
            pltpu.SMEM((6, 4, NLEAF), jnp.int32),
            pltpu.SMEM((8, LEAVES), jnp.int32),
            vmem((LEAVES, COLS, WIDTH), BF16),
            vmem((SLOTS, NRHS * COLS, WIDTH), BF16),
            vmem((6, 4, COLS, WIDTH), BF16),
            vmem((32, LEAVES * WIDTH), F32),
            vmem((LEAVES, 2, WIDTH, WIDTH), BF16),
            vmem((LEAVES, 8, 32, 32), F32),
            vmem((1024, 64), F32),
            vmem((1024, 128), F32),
            vmem((3, 1024, 128), F32),
            vmem((512, 128), F32),
            vmem((1024, 128), F32),
            vmem((3072, 128), F32),
            vmem((64, 32, 128), BF16),
            vmem((LEAVES, 32, 128), BF16),
            vmem((LEAVES, 32, 128), BF16),
            vmem((LEAVES, 32, 128), BF16),
            vmem((LEAVES, 32, 128), BF16),
            vmem((64, 32, 128), BF16),
            vmem((LEAVES, COLS, 128), F32),
            vmem((LEAVES, COLS, 128), F32),
            vmem((64, 32, 128), F32),
            vmem((32, 32, 128), BF16),
            vmem((32, 32, 128), BF16),
            vmem((COLS, 128), BF16),
            vmem((COLS, 128), BF16),
            vmem((4, COLS, 128), BF16),
            vmem((32, COLS, 128), BF16),
            vmem((NRHS, LEAVES, COLS, WIDTH), F32),
            vmem((2, 16, COLS, WIDTH), F32),
            vmem((2, LEAVES, COLS, WIDTH), F32),
            dma((LEAVES,)),
            dma((9,)),
            dma((6,)),
            dma((6,)),
            dma((6,)),
            dma((6,)),
            dma((6,)),
            dma((6,)),
            dma((4,)),
            dma((4,)),
            dma((31,)),
            dma((31,)),
            dma((10,)),
            dma((10,)),
        ],
        compiler_params=pltpu.CompilerParams(
            collective_id=0, has_side_effects=True, vmem_limit_bytes=60 * 2**20
        ),
        name="h2_product",
    )(
        dens,
        bases,
        blocks,
        near_src.T,
        send_leaf.transpose(1, 2, 0),
        far_src.T,
        coupling,
        local_t[0].transpose(1, 2, 0).reshape(1024, 64),
        upper_t.transpose(1, 2, 0).reshape(1024, 128),
        up_c.transpose(1, 2, 3, 0).reshape(3, 1024, 128),
    )


def solution(mesh):
    in_specs = (
        P("rhs", "leaf"),
        P(None, "leaf"),
        P("leaf", "rhs", None, None),
        P("leaf", "rhs"),
        P(),
        P("leaf", None),
        P("leaf", None, None, None),
        P("leaf", None, None, None),
        P(),
        P(),
    )
    return jax.shard_map(
        local, mesh=mesh, in_specs=in_specs, out_specs=P("rhs", "leaf"), check_vma=False
    )
```

```python
import functools

import jax
import jax.numpy as jnp
from jax import lax
from jax.experimental import pallas as pl
from jax.experimental.pallas import tpu as pltpu
from jax.sharding import PartitionSpec as P

F32 = jnp.float32
BF16 = jnp.bfloat16
MESH = pl.DeviceIdType.MESH
LEAVES = 32
WIDTH = 128
COLS = 16
NLEAF = 64
NRHS = 4
SLOTS = 56
FACES = (1, -1, 4, -4, 16, -16)
GREET = tuple(range(1, 9)) + (16, 24)


def dot_nn(a, b):
    return lax.dot_general(a, b, (((1,), (0,)), ((), ())), preferred_element_type=F32)


def dot_nt(a, b):
    return lax.dot_general(a, b, (((1,), (1,)), ((), ())), preferred_element_type=F32)


def halves(x):
    high = x.astype(BF16)
    return high, (x - high.astype(F32)).astype(BF16)


def lane_group(shape):
    return lax.broadcasted_iota(jnp.int32, shape, len(shape) - 1) // 32


def coef_form(r):
    group = lane_group(r.shape)
    high = r.astype(BF16).astype(F32)
    return jnp.where(group % 2 == 0, high, r - high).astype(BF16)


def unfold(tile):
    group = lane_group(tile.shape)
    turned = [tile] + [pltpu.roll(tile, 32 * k, 1) for k in (1, 2, 3)]
    rows = []
    for b in range(4):
        pick = [turned[(g - b) % 4] for g in range(4)]
        rows.append(
            jnp.where(
                group < 2,
                jnp.where(group == 0, pick[0], pick[1]),
                jnp.where(group == 2, pick[2], pick[3]),
            )
        )
    return jnp.concatenate(rows, axis=0)


def rows_form(high, low):
    return jnp.concatenate([high, high, low, low], axis=0)


def lanes_form(m):
    high = m.astype(BF16).astype(F32)
    v = jnp.where(lane_group(m.shape) < 2, high, m - high).astype(BF16)
    return jnp.concatenate([v] * 4, axis=0)


def kernel(
    dens,
    bases,
    blocks,
    nsrc_h,
    sleaf_h,
    fsrc_h,
    coup,
    loc_t,
    up_t,
    up_c,
    out,
    nsrc,
    sleaf,
    fsrc,
    own,
    buf,
    stage,
    bas_v,
    blk_v,
    cpl_v,
    loc_v,
    upt_v,
    upc_v,
    ef,
    uf,
    cf,
    e_v,
    b_hi,
    b_lo,
    q_hi,
    q_lo,
    t_x,
    f_rep,
    acc,
    m_rep,
    m_hi,
    m_lo,
    root_x,
    pair_x,
    lrecv,
    chips,
    part,
    raw,
    rbuf,
    own_sem,
    loc_sem,
    os_sem,
    or_sem,
    hs_sem,
    hr_sem,
    ys_sem,
    yr_sem,
    ls_sem,
    lr_sem,
    gs_sem,
    gr_sem,
    ps_sem,
    pr_sem,
    news,
):
    d = lax.axis_index("leaf")
    me = lax.axis_index("rhs")

    def leaf_at(offset):
        return lax.rem(d + (offset + 2 * NLEAF), NLEAF)

    def rhs_at(offset):
        return lax.rem(me + offset, NRHS)

    right, across, left = rhs_at(1), rhs_at(2), rhs_at(3)

    def rows_of(r):
        return pl.ds(pl.multiple_of(r * COLS, COLS), COLS)

    my_rows = rows_of(me)

    def inside(offset):
        if offset > 0:
            return d < NLEAF - offset
        return d >= -offset

    def greet(sem, offsets):
        count = 0
        for offset in offsets:
            for o in (offset, -offset):
                count = count + jnp.where(inside(o), 1, 0)

                @pl.when(inside(o))
                def _():
                    pl.semaphore_signal(
                        sem, inc=1, device_id={"leaf": d + o}, device_id_type=MESH
                    )

        return count

    for k in range(LEAVES, SLOTS):
        buf[k, my_rows, :] = jnp.zeros((COLS, WIDTH), BF16)

    barrier = pltpu.get_barrier_semaphore()
    for peer in (right, left):
        pl.semaphore_signal(barrier, inc=1, device_id={"rhs": peer}, device_id_type=MESH)
    greeted = greet(barrier, GREET)

    def own_copy(k):
        return pltpu.make_async_copy(
            dens.at[:, pl.ds(pl.multiple_of(k * WIDTH, WIDTH), WIDTH)], own.at[k], own_sem.at[k]
        )

    pairs = (
        (loc_t, loc_v),
        (bases, bas_v),
        (sleaf_h, sleaf),
        (up_t, upt_v),
        (coup, cpl_v),
        (fsrc_h, fsrc),
        (blocks, blk_v),
        (nsrc_h, nsrc),
        (up_c, upc_v),
    )
    loads = [pltpu.make_async_copy(s, v, loc_sem.at[i]) for i, (s, v) in enumerate(pairs)]
    for load in loads[:3]:
        load.start()

    @pl.loop(0, LEAVES)
    def _(k):
        own_copy(k).start()

    for load in loads[3:]:
        load.start()

    loads[0].wait()
    for a in range(8):
        blk = jnp.concatenate([loc_v[pl.ds(32 * (8 * b + a), 32), :] for b in range(4)], axis=0)
        ef[pl.ds(64 * a, 64), :] = blk.T

    @pl.loop(0, 64, unroll=8)
    def _(n):
        m = unfold(ef[pl.ds(n, 8, stride=64), :])
        high = m.astype(BF16).astype(F32)
        e_v[n] = jnp.where(lane_group(m.shape) < 2, high, m - high).astype(BF16)

    row = lax.broadcasted_iota(jnp.int32, (32, 128), 0)
    lane = lax.broadcasted_iota(jnp.int32, (32, 128), 1)
    t_x[1] = jnp.where((lane % 64) == row, 1.0, 0.0).astype(BF16)
    for width in (2, 4, 8, 16, 32):
        for p in range(width // 2, width):
            w = jnp.concatenate([e_v[2 * p], e_v[2 * p + 1]], axis=0)
            r = dot_nt(t_x[p], w)
            t_x[2 * p] = coef_form(jnp.concatenate([r[:, :32]] * 4, axis=1))
            t_x[2 * p + 1] = coef_form(jnp.concatenate([r[:, 32:]] * 4, axis=1))

    @pl.loop(0, LEAVES)
    def _(k):
        own_copy(k).wait()

    loads[2].wait()
    for j in range(6):
        for c in range(4):
            wanted = jnp.maximum(sleaf[j, c, d], 0)
            stage[j, c] = own[wanted]

    @pl.loop(0, LEAVES, unroll=8)
    def _(k):
        buf[k, my_rows, :] = own[k]

    pl.semaphore_wait(barrier, 2 + greeted)

    near_planes = greet(news.at[0], (8, 16, 24))

    side = 1 - 2 * lax.rem(d, 2)
    third = d + 3 * side
    third_ok = (third >= 0) & (third < NLEAF)
    partners = (d + 2, d - 2, third, d + side)
    root_out_ok = (inside(2), inside(-2), third_ok)
    root_in_ok = (inside(-2), inside(2), third_ok)
    root_sends = [
        pltpu.make_async_remote_copy(
            src_ref=root_x,
            dst_ref=lrecv.at[i],
            send_sem=ls_sem.at[i],
            recv_sem=lr_sem.at[i],
            device_id={"leaf": partner},
            device_id_type=MESH,
        )
        for i, partner in enumerate(partners)
    ]
    halo_sends = [
        pltpu.make_async_remote_copy(
            src_ref=stage.at[j],
            dst_ref=buf.at[pl.ds(LEAVES + 4 * j, 4), my_rows, :],
            send_sem=hs_sem.at[j],
            recv_sem=hr_sem.at[j],
            device_id={"leaf": d + FACES[j]},
            device_id_type=MESH,
        )
        for j in range(6)
    ]

    def over_rhs(src, dst, target, ssem, rsem):
        return pltpu.make_async_remote_copy(
            src_ref=src,
            dst_ref=dst,
            send_sem=ssem,
            recv_sem=rsem,
            device_id={"rhs": target},
            device_id_type=MESH,
        )

    def pass_on(slots, target, source, index, ssem, rsem):
        piece = buf.at[slots, rows_of(source), :]
        return over_rhs(piece, piece, target, ssem.at[index], rsem.at[index])

    lower, upper = pl.ds(0, 16), pl.ds(16, 16)
    own_out = [
        over_rhs(own.at[lower], buf.at[lower, my_rows, :], right, os_sem.at[0], or_sem.at[0]),
        over_rhs(own.at[upper], buf.at[upper, my_rows, :], left, os_sem.at[1], or_sem.at[1]),
        over_rhs(own.at[upper], buf.at[upper, my_rows, :], right, os_sem.at[2], or_sem.at[2]),
        over_rhs(own.at[lower], buf.at[lower, my_rows, :], left, os_sem.at[3], or_sem.at[3]),
    ]
    own_relay = [
        pass_on(lower, right, left, 4, os_sem, or_sem),
        pass_on(upper, left, right, 5, os_sem, or_sem),
    ]
    first, second = pl.ds(LEAVES, 12), pl.ds(LEAVES + 12, 12)
    halo_out = [
        pass_on(first, right, me, 0, ys_sem, yr_sem),
        pass_on(second, left, me, 1, ys_sem, yr_sem),
        pass_on(second, right, me, 2, ys_sem, yr_sem),
        pass_on(first, left, me, 3, ys_sem, yr_sem),
    ]
    halo_relay = [
        pass_on(first, right, left, 4, ys_sem, yr_sem),
        pass_on(second, left, right, 5, ys_sem, yr_sem),
    ]
    for j in range(6):
        pl.when(inside(FACES[j]))(halo_sends[j].start)
    for send in own_out:
        send.start()

    loads[1].wait()

    @pl.loop(0, LEAVES, unroll=8)
    def _(t):
        high, low = halves(bas_v[:, pl.ds(pl.multiple_of(t * WIDTH, WIDTH), WIDTH)])
        b_hi[t] = high
        b_lo[t] = low
        high, low = halves(dot_nn(t_x[LEAVES + t], rows_form(high, low)))
        q_hi[t] = high
        q_lo[t] = low

    root = jnp.zeros((COLS, 32), F32)
    for t in range(LEAVES):
        x = own[t]
        root = root + dot_nt(
            jnp.concatenate([x, x], axis=1), jnp.concatenate([q_hi[t], q_lo[t]], axis=1)
        )
    root_x[...] = coef_form(jnp.concatenate([root] * 4, axis=1))
    root_sends[3].start()
    for i in range(3):
        pl.when(root_out_ok[i])(root_sends[i].start)

        @pl.when(jnp.logical_not(root_in_ok[i]))
        def _():
            lrecv[i] = jnp.zeros((COLS, 128), BF16)

    @pl.loop(0, LEAVES, unroll=8)
    def _(t):
        w = jnp.concatenate([b_hi[t], b_lo[t]], axis=1)
        x = own[t]
        r = dot_nt(jnp.concatenate([x, x], axis=1), w)
        f_rep[t] = jnp.concatenate([r] * 4, axis=1)

    for j in range(6):
        pl.when(inside(-FACES[j]))(halo_sends[j].wait_recv)
    for send in halo_out:
        send.start()
    for send in own_out[:2]:
        send.wait_recv()
    for send in own_relay:
        send.start()

    loads[3].wait()
    for a in range(8):
        blk = jnp.concatenate([upt_v[pl.ds(32 * (8 * b + a), 32), :] for b in range(4)], axis=0)
        uf[pl.ds(128 * a, 128), :] = blk.T

    def above(n):
        return unfold(uf[pl.ds(n, 8, stride=128), :])

    n0 = d + NLEAF
    chip = lax.div(d, 2)

    def leaf_coupling(begin, count):
        @pl.loop(begin, begin + count, unroll=8)
        def _(t):
            group = lane_group((COLS, 128))
            x_high, x_low, c_high, c_low = [], [], [], []
            for half in range(2):
                g = [f_rep[fsrc[4 * half + j, t]] for j in range(4)]
                g = jnp.where(
                    group < 2,
                    jnp.where(group == 0, g[0], g[1]),
                    jnp.where(group == 2, g[2], g[3]),
                )
                high, low = halves(g)
                x_high.append(high)
                x_low.append(low)
                m = jnp.concatenate([cpl_v[t, 4 * half + j] for j in range(4)], axis=1)
                high, low = halves(m)
                c_high.append(high)
                c_low.append(low)
            x = jnp.concatenate(x_high + x_low + x_high, axis=1)
            w = jnp.concatenate(c_high + c_high + c_low, axis=1)
            r = dot_nt(x, w)
            x = coef_form(jnp.concatenate([r] * 4, axis=1))
            acc[t] = dot_nn(x, rows_form(b_hi[t], b_lo[t]))

    root_sends[3].wait_recv()
    x = jnp.concatenate([root_x[...], lrecv[3]], axis=1)
    w = jnp.concatenate(
        [rows_form(*halves(above(n0))), rows_form(*halves(above(n0 + side)))], axis=0
    )
    pair = coef_form(dot_nn(x, w))
    pair_x[...] = pair
    chips[chip] = pair
    chip_sends = [
        pltpu.make_async_remote_copy(
            src_ref=pair_x,
            dst_ref=chips.at[chip],
            send_sem=gs_sem.at[k - 1],
            recv_sem=gr_sem.at[k - 1],
            device_id={"leaf": leaf_at(2 * k)},
            device_id_type=MESH,
        )
        for k in range(1, 32)
    ]
    pl.semaphore_wait(news.at[0], near_planes)
    far_planes = greet(news.at[1], (32,))

    loads[4].wait()
    loads[5].wait()
    leaf_coupling(0, 8)

    for send in halo_out[:2]:
        send.wait_recv()
    for send in halo_relay:
        send.start()

    pl.semaphore_wait(news.at[1], far_planes)
    for send in chip_sends:
        send.start()

    loads[6].wait()
    loads[7].wait()
    for send in own_out[2:] + own_relay + halo_out[2:] + halo_relay:
        send.wait_recv()

    def near(begin, count):
        @pl.loop(begin, begin + count, unroll=8)
        def _(t):
            x = jnp.concatenate([buf[nsrc[0, t]], buf[nsrc[1, t]]], axis=1)
            w = jnp.concatenate([blk_v[t, 0], blk_v[t, 1]], axis=1)
            o = dot_nt(x, w)
            for q in range(NRHS):
                part[q, t] = o[COLS * q : COLS * (q + 1)]

    def partial(index, dest, t0, count, target, landing):
        return over_rhs(
            part.at[dest, pl.ds(t0, count)], landing, target, ps_sem.at[index], pr_sem.at[index]
        )

    raw_sends = [
        partial(0, across, 0, 8, right, raw.at[0, pl.ds(0, 8)]),
        partial(1, across, 16, 8, left, raw.at[1, pl.ds(0, 8)]),
        partial(2, across, 8, 8, right, raw.at[0, pl.ds(8, 8)]),
        partial(3, across, 24, 8, left, raw.at[1, pl.ds(8, 8)]),
    ]
    plain_sends = [
        partial(4, right, 16, 16, right, rbuf.at[0, upper]),
        partial(5, left, 0, 16, left, rbuf.at[1, lower]),
    ]
    sum_sends = [
        partial(6, right, 0, 8, right, rbuf.at[0, pl.ds(0, 8)]),
        partial(7, left, 16, 8, left, rbuf.at[1, pl.ds(16, 8)]),
        partial(8, right, 8, 8, right, rbuf.at[0, pl.ds(8, 8)]),
        partial(9, left, 24, 8, left, rbuf.at[1, pl.ds(24, 8)]),
    ]
    for i, begin in enumerate((0, 16, 8, 24)):
        near(begin, 8)
        raw_sends[i].start()
    for send in plain_sends:
        send.start()

    def join(i):
        side_of, begin = ((0, 0), (1, 16), (0, 8), (1, 24))[i]
        dest = left if side_of else right
        raw_sends[i].wait_recv()

        @pl.loop(0, 8, unroll=8)
        def _(k):
            t = begin + k
            part[dest, t] = part[dest, t] + raw[side_of, t - 16 * side_of]

        sum_sends[i].start()

    loads[8].wait()
    for c in range(3):
        for a in range(8):
            blk = jnp.concatenate(
                [upc_v[c, pl.ds(8 * b + a, 32, stride=32), :] for b in range(4)], axis=0
            )
            cf[pl.ds(1024 * c + 128 * a, 128), :] = blk.T

    join(0)
    join(1)

    down = None
    couplings = {}
    for level in range(5):
        n = lax.div(n0, 2**level)
        width = NLEAF // 2**level
        t = n - width
        even = lax.rem(t, 2) == 0
        valid = (t >= 2, t + 2 < width, jnp.where(even, t + 3 < width, t >= 3))
        where_to = (n - 2, n + 2, n + 3 - 6 * lax.rem(t, 2))
        cts = []
        for c in range(3):
            ct = unfold(cf[pl.ds(1024 * c + n, 8, stride=128), :])
            cts.append(ct * valid[c].astype(F32))
        if level:
            left_side = jnp.concatenate([coef_form(ct) for ct in cts], axis=0)
            r = dot_nt(left_side, lanes_form(down))
            cts = [r[32 * c : 32 * (c + 1)] for c in range(3)]
        couplings[level] = [
            (jnp.where(ok, place, n), ct) for ok, place, ct in zip(valid, where_to, cts)
        ]
        if level == 0:
            down = above(n0)
        elif level < 4:
            down = dot_nn(coef_form(down), rows_form(*halves(above(n))))

    leaf_coupling(8, 8)

    join(2)
    join(3)

    leaf_coupling(16, 16)

    for n in range(4, 8):
        m_rep[n] = jnp.zeros((32, 128), F32)
    for level in (4, 3, 2, 1):
        width = NLEAF // 2**level
        if level < 4:
            for p in range(width // 2, width):
                lhs = jnp.concatenate(
                    [coef_form(above(2 * p)), coef_form(above(2 * p + 1))], axis=0
                )
                r = dot_nn(lhs, rows_form(*halves(m_rep[p])))
                m_rep[2 * p] = r[:32]
                m_rep[2 * p + 1] = r[32:]
        for place, ct in couplings[level]:
            m_rep[place] = m_rep[place] + ct

    @pl.loop(0, 32, unroll=4)
    def _(e):
        high, low = halves(m_rep[32 + e])
        m_hi[e] = high
        m_lo[e] = low

    for i in range(3):
        pl.when(root_in_ok[i])(root_sends[i].wait_recv)
    field = jnp.zeros((COLS, 128), F32)
    for c in range(3):
        field = field + dot_nn(lrecv[c], rows_form(*halves(couplings[0][c][1])))
    for send in chip_sends:
        send.wait_recv()
    for e in range(0, 32, 2):
        x = jnp.concatenate([chips[e], chips[e + 1]], axis=1)
        w = jnp.concatenate(
            [rows_form(m_hi[e], m_lo[e]), rows_form(m_hi[e + 1], m_lo[e + 1])], axis=0
        )
        field = field + dot_nn(x, w)
    field_x = coef_form(field)

    @pl.loop(0, LEAVES, unroll=8)
    def _(t):
        acc[t] = acc[t] + dot_nn(field_x, rows_form(q_hi[t], q_lo[t]))

    for send in plain_sends:
        send.wait_recv()
    for i, begin in enumerate((0, 16, 8, 24)):
        sum_sends[i].wait_recv()

        @pl.loop(begin, begin + 8, unroll=8)
        def _(t):
            near_sum = part[me, t] + (rbuf[0, t] + rbuf[1, t])
            out[:, pl.ds(pl.multiple_of(t * WIDTH, WIDTH), WIDTH)] = near_sum + acc[t]

    for j in range(6):
        pl.when(inside(FACES[j]))(halo_sends[j].wait_send)
    for i in range(3):
        pl.when(root_out_ok[i])(root_sends[i].wait_send)
    for send in root_sends[3:] + own_out + own_relay + halo_out + halo_relay:
        send.wait_send()
    for send in chip_sends + raw_sends + plain_sends + sum_sends:
        send.wait_send()


def local(dens, bases, blocks, near_src, send_leaf, far_src, coupling, local_t, upper_t, up_c):
    any_spec = pl.BlockSpec(memory_space=pltpu.HBM)
    dma = pltpu.SemaphoreType.DMA
    vmem = pltpu.VMEM
    return pl.pallas_call(
        kernel,
        out_shape=jax.ShapeDtypeStruct((COLS, LEAVES * WIDTH), F32),
        in_specs=[any_spec] * 10,
        out_specs=pl.BlockSpec(memory_space=pltpu.VMEM),
        scratch_shapes=[
            pltpu.SMEM((2, LEAVES), jnp.int32),
            pltpu.SMEM((6, 4, NLEAF), jnp.int32),
            pltpu.SMEM((8, LEAVES), jnp.int32),
            vmem((LEAVES, COLS, WIDTH), BF16),
            vmem((SLOTS, NRHS * COLS, WIDTH), BF16),
            vmem((6, 4, COLS, WIDTH), BF16),
            vmem((32, LEAVES * WIDTH), F32),
            vmem((LEAVES, 2, WIDTH, WIDTH), BF16),
            vmem((LEAVES, 8, 32, 32), F32),
            vmem((1024, 64), F32),
            vmem((1024, 128), F32),
            vmem((3, 1024, 128), F32),
            vmem((512, 128), F32),
            vmem((1024, 128), F32),
            vmem((3072, 128), F32),
            vmem((64, 32, 128), BF16),
            vmem((LEAVES, 32, 128), BF16),
            vmem((LEAVES, 32, 128), BF16),
            vmem((LEAVES, 32, 128), BF16),
            vmem((LEAVES, 32, 128), BF16),
            vmem((64, 32, 128), BF16),
            vmem((LEAVES, COLS, 128), F32),
            vmem((LEAVES, COLS, 128), F32),
            vmem((64, 32, 128), F32),
            vmem((32, 32, 128), BF16),
            vmem((32, 32, 128), BF16),
            vmem((COLS, 128), BF16),
            vmem((COLS, 128), BF16),
            vmem((4, COLS, 128), BF16),
            vmem((32, COLS, 128), BF16),
            vmem((NRHS, LEAVES, COLS, WIDTH), F32),
            vmem((2, 16, COLS, WIDTH), F32),
            vmem((2, LEAVES, COLS, WIDTH), F32),
            dma((LEAVES,)),
            dma((9,)),
            dma((6,)),
            dma((6,)),
            dma((6,)),
            dma((6,)),
            dma((6,)),
            dma((6,)),
            dma((4,)),
            dma((4,)),
            dma((31,)),
            dma((31,)),
            dma((10,)),
            dma((10,)),
            pltpu.SemaphoreType.REGULAR((2,)),
        ],
        compiler_params=pltpu.CompilerParams(
            collective_id=0, has_side_effects=True, vmem_limit_bytes=48 * 2**20
        ),
        name="h2_product",
    )(
        *(
            pltpu.with_memory_space_constraint(x, pltpu.HBM)
            for x in (
        dens,
        bases,
        blocks,
        near_src.T,
        send_leaf.transpose(1, 2, 0),
        far_src.T,
        coupling,
        local_t[0].transpose(1, 2, 0).reshape(1024, 64),
        upper_t.transpose(1, 2, 0).reshape(1024, 128),
        up_c.transpose(1, 2, 3, 0).reshape(3, 1024, 128),
            )
        )
    )


def solution(mesh):
    in_specs = (
        P("rhs", "leaf"),
        P(None, "leaf"),
        P("leaf", "rhs", None, None),
        P("leaf", "rhs"),
        P(),
        P("leaf", None),
        P("leaf", None, None, None),
        P("leaf", None, None, None),
        P(),
        P(),
    )
    return jax.shard_map(
        local, mesh=mesh, in_specs=in_specs, out_specs=P("rhs", "leaf"), check_vma=False
    )
```

```python
import functools

import jax
import jax.numpy as jnp
from jax import lax
from jax.experimental import pallas as pl
from jax.experimental.pallas import tpu as pltpu
from jax.sharding import PartitionSpec as P

F32 = jnp.float32
BF16 = jnp.bfloat16
MESH = pl.DeviceIdType.MESH
LEAVES = 32
WIDTH = 128
COLS = 16
NLEAF = 64
NRHS = 4
SLOTS = 56
FACES = (1, -1, 4, -4, 16, -16)
GREET = tuple(range(1, 9)) + (16, 24)


def dot_nn(a, b):
    return lax.dot_general(a, b, (((1,), (0,)), ((), ())), preferred_element_type=F32)


def dot_nt(a, b):
    return lax.dot_general(a, b, (((1,), (1,)), ((), ())), preferred_element_type=F32)


def halves(x):
    high = x.astype(BF16)
    return high, (x - high.astype(F32)).astype(BF16)


def lane_group(shape):
    return lax.broadcasted_iota(jnp.int32, shape, len(shape) - 1) // 32


def coef_form(r):
    group = lane_group(r.shape)
    high = r.astype(BF16).astype(F32)
    return jnp.where(group % 2 == 0, high, r - high).astype(BF16)


def unfold(tile):
    group = lane_group(tile.shape)
    turned = [tile] + [pltpu.roll(tile, 32 * k, 1) for k in (1, 2, 3)]
    rows = []
    for b in range(4):
        pick = [turned[(g - b) % 4] for g in range(4)]
        rows.append(
            jnp.where(
                group < 2,
                jnp.where(group == 0, pick[0], pick[1]),
                jnp.where(group == 2, pick[2], pick[3]),
            )
        )
    return jnp.concatenate(rows, axis=0)


def rows_form(high, low):
    return jnp.concatenate([high, high, low, low], axis=0)


def lanes_form(m):
    high = m.astype(BF16).astype(F32)
    v = jnp.where(lane_group(m.shape) < 2, high, m - high).astype(BF16)
    return jnp.concatenate([v] * 4, axis=0)


def kernel(
    dens,
    bases,
    blocks,
    nsrc_h,
    sleaf_h,
    fsrc_h,
    coup,
    loc_t,
    up_t,
    up_c,
    out,
    nsrc,
    sleaf,
    fsrc,
    own,
    buf,
    stage,
    bas_v,
    blk_v,
    cpl_v,
    loc_v,
    upt_v,
    upc_v,
    ef,
    uf,
    cf,
    e_v,
    b_hi,
    b_lo,
    q_hi,
    q_lo,
    t_x,
    f_rep,
    ll_x,
    acc,
    m_rep,
    m_hi,
    m_lo,
    root_x,
    pair_x,
    lrecv,
    chips,
    part,
    raw,
    rbuf,
    own_sem,
    loc_sem,
    os_sem,
    or_sem,
    hs_sem,
    hr_sem,
    ys_sem,
    yr_sem,
    ls_sem,
    lr_sem,
    gs_sem,
    gr_sem,
    ps_sem,
    pr_sem,
    news,
):
    d = lax.axis_index("leaf")
    me = lax.axis_index("rhs")

    def leaf_at(offset):
        return lax.rem(d + (offset + 2 * NLEAF), NLEAF)

    def rhs_at(offset):
        return lax.rem(me + offset, NRHS)

    right, across, left = rhs_at(1), rhs_at(2), rhs_at(3)

    def rows_of(r):
        return pl.ds(pl.multiple_of(r * COLS, COLS), COLS)

    my_rows = rows_of(me)

    def inside(offset):
        if offset > 0:
            return d < NLEAF - offset
        return d >= -offset

    def greet(sem, offsets):
        count = 0
        for offset in offsets:
            for o in (offset, -offset):
                count = count + jnp.where(inside(o), 1, 0)

                @pl.when(inside(o))
                def _():
                    pl.semaphore_signal(
                        sem, inc=1, device_id={"leaf": d + o}, device_id_type=MESH
                    )

        return count

    for k in range(LEAVES, SLOTS):
        buf[k, my_rows, :] = jnp.zeros((COLS, WIDTH), BF16)

    barrier = pltpu.get_barrier_semaphore()
    for peer in (right, left):
        pl.semaphore_signal(barrier, inc=1, device_id={"rhs": peer}, device_id_type=MESH)
    greeted = greet(barrier, GREET)

    def own_copy(k):
        return pltpu.make_async_copy(
            dens.at[:, pl.ds(pl.multiple_of(k * WIDTH, WIDTH), WIDTH)], own.at[k], own_sem.at[k]
        )

    pairs = (
        (loc_t, loc_v),
        (bases, bas_v),
        (sleaf_h, sleaf),
        (up_t, upt_v),
        (coup, cpl_v),
        (fsrc_h, fsrc),
        (blocks, blk_v),
        (nsrc_h, nsrc),
        (up_c, upc_v),
    )
    loads = [pltpu.make_async_copy(s, v, loc_sem.at[i]) for i, (s, v) in enumerate(pairs)]
    for load in loads[:3]:
        load.start()

    @pl.loop(0, LEAVES)
    def _(k):
        own_copy(k).start()

    for load in loads[3:]:
        load.start()

    loads[0].wait()
    for a in range(8):
        blk = jnp.concatenate([loc_v[pl.ds(32 * (8 * b + a), 32), :] for b in range(4)], axis=0)
        ef[pl.ds(64 * a, 64), :] = blk.T

    @pl.loop(0, 64, unroll=8)
    def _(n):
        m = unfold(ef[pl.ds(n, 8, stride=64), :])
        high = m.astype(BF16).astype(F32)
        e_v[n] = jnp.where(lane_group(m.shape) < 2, high, m - high).astype(BF16)

    row = lax.broadcasted_iota(jnp.int32, (32, 128), 0)
    lane = lax.broadcasted_iota(jnp.int32, (32, 128), 1)
    t_x[1] = jnp.where((lane % 64) == row, 1.0, 0.0).astype(BF16)
    for width in (2, 4, 8, 16, 32):
        for p in range(width // 2, width):
            w = jnp.concatenate([e_v[2 * p], e_v[2 * p + 1]], axis=0)
            r = dot_nt(t_x[p], w)
            t_x[2 * p] = coef_form(jnp.concatenate([r[:, :32]] * 4, axis=1))
            t_x[2 * p + 1] = coef_form(jnp.concatenate([r[:, 32:]] * 4, axis=1))

    @pl.loop(0, LEAVES)
    def _(k):
        own_copy(k).wait()

    loads[2].wait()
    for j in range(6):
        for c in range(4):
            wanted = jnp.maximum(sleaf[j, c, d], 0)
            stage[j, c] = own[wanted]

    @pl.loop(0, LEAVES, unroll=8)
    def _(k):
        buf[k, my_rows, :] = own[k]

    pl.semaphore_wait(barrier, 2 + greeted)

    near_planes = greet(news.at[0], (8, 16, 24))

    side = 1 - 2 * lax.rem(d, 2)
    third = d + 3 * side
    third_ok = (third >= 0) & (third < NLEAF)
    partners = (d + 2, d - 2, third, d + side)
    root_out_ok = (inside(2), inside(-2), third_ok)
    root_in_ok = (inside(-2), inside(2), third_ok)
    root_sends = [
        pltpu.make_async_remote_copy(
            src_ref=root_x,
            dst_ref=lrecv.at[i],
            send_sem=ls_sem.at[i],
            recv_sem=lr_sem.at[i],
            device_id={"leaf": partner},
            device_id_type=MESH,
        )
        for i, partner in enumerate(partners)
    ]
    halo_sends = [
        pltpu.make_async_remote_copy(
            src_ref=stage.at[j],
            dst_ref=buf.at[pl.ds(LEAVES + 4 * j, 4), my_rows, :],
            send_sem=hs_sem.at[j],
            recv_sem=hr_sem.at[j],
            device_id={"leaf": d + FACES[j]},
            device_id_type=MESH,
        )
        for j in range(6)
    ]

    def over_rhs(src, dst, target, ssem, rsem):
        return pltpu.make_async_remote_copy(
            src_ref=src,
            dst_ref=dst,
            send_sem=ssem,
            recv_sem=rsem,
            device_id={"rhs": target},
            device_id_type=MESH,
        )

    def pass_on(slots, target, source, index, ssem, rsem):
        piece = buf.at[slots, rows_of(source), :]
        return over_rhs(piece, piece, target, ssem.at[index], rsem.at[index])

    lower, upper = pl.ds(0, 16), pl.ds(16, 16)
    own_out = [
        over_rhs(own.at[lower], buf.at[lower, my_rows, :], right, os_sem.at[0], or_sem.at[0]),
        over_rhs(own.at[upper], buf.at[upper, my_rows, :], left, os_sem.at[1], or_sem.at[1]),
        over_rhs(own.at[upper], buf.at[upper, my_rows, :], right, os_sem.at[2], or_sem.at[2]),
        over_rhs(own.at[lower], buf.at[lower, my_rows, :], left, os_sem.at[3], or_sem.at[3]),
    ]
    own_relay = [
        pass_on(lower, right, left, 4, os_sem, or_sem),
        pass_on(upper, left, right, 5, os_sem, or_sem),
    ]
    first, second = pl.ds(LEAVES, 12), pl.ds(LEAVES + 12, 12)
    halo_out = [
        pass_on(first, right, me, 0, ys_sem, yr_sem),
        pass_on(second, left, me, 1, ys_sem, yr_sem),
        pass_on(second, right, me, 2, ys_sem, yr_sem),
        pass_on(first, left, me, 3, ys_sem, yr_sem),
    ]
    halo_relay = [
        pass_on(first, right, left, 4, ys_sem, yr_sem),
        pass_on(second, left, right, 5, ys_sem, yr_sem),
    ]
    for j in range(6):
        pl.when(inside(FACES[j]))(halo_sends[j].start)
    for send in own_out:
        send.start()

    loads[1].wait()

    @pl.loop(0, LEAVES, step=2, unroll=4)
    def _(t):
        maps = []
        for k in range(2):
            lanes = pl.ds(pl.multiple_of((t + k) * WIDTH, WIDTH), WIDTH)
            b_hi[t + k], b_lo[t + k] = pair = halves(bas_v[:, lanes])
            maps.append(rows_form(*pair))
        x = jnp.concatenate([t_x[LEAVES + t], t_x[LEAVES + t + 1]], axis=0)
        r = dot_nn(x, jnp.concatenate(maps, axis=1))
        for k in range(2):
            q_hi[t + k], q_lo[t + k] = halves(r[32 * k : 32 * k + 32, 128 * k : 128 * k + 128])

    root = jnp.zeros((COLS, 64), F32)
    for t in range(0, LEAVES, 2):
        x = jnp.concatenate([own[t], own[t + 1]], axis=1)
        w = jnp.concatenate(
            [
                jnp.concatenate([q_hi[t], q_hi[t + 1]], axis=1),
                jnp.concatenate([q_lo[t], q_lo[t + 1]], axis=1),
            ],
            axis=0,
        )
        root = root + dot_nt(x, w)
    root = root[:, :32] + root[:, 32:]
    root_x[...] = coef_form(jnp.concatenate([root] * 4, axis=1))
    root_sends[3].start()
    for i in range(3):
        pl.when(root_out_ok[i])(root_sends[i].start)

        @pl.when(jnp.logical_not(root_in_ok[i]))
        def _():
            lrecv[i] = jnp.zeros((COLS, 128), BF16)

    pl.semaphore_wait(news.at[0], near_planes)
    far_planes = greet(news.at[1], (32,))

    @pl.loop(0, LEAVES, step=4, unroll=4)
    def _(t):
        w = jnp.concatenate([m[t + k] for k in range(4) for m in (b_hi, b_lo)], axis=0)
        r = dot_nt(jnp.concatenate([own[t + k] for k in range(4)], axis=0), w)
        for k in range(4):
            v = r[COLS * k : COLS * (k + 1), 64 * k : 64 * (k + 1)]
            f_rep[t + k] = jnp.concatenate([v[:, :32] + v[:, 32:]] * 4, axis=1)

    for j in range(6):
        pl.when(inside(-FACES[j]))(halo_sends[j].wait_recv)
    for send in halo_out:
        send.start()
    for send in own_out[:2]:
        send.wait_recv()
    for send in own_relay:
        send.start()

    loads[3].wait()
    for a in range(8):
        blk = jnp.concatenate([upt_v[pl.ds(32 * (8 * b + a), 32), :] for b in range(4)], axis=0)
        uf[pl.ds(128 * a, 128), :] = blk.T

    def above(n):
        return unfold(uf[pl.ds(n, 8, stride=128), :])

    n0 = d + NLEAF
    chip = lax.div(d, 2)

    def leaf_coupling(begin, count):
        @pl.loop(begin, begin + count, step=4, unroll=2)
        def _(t):
            group = lane_group((COLS, 128))
            xs, ws = [], []
            for k in range(4):
                x, w = [], []
                for half in range(2):
                    g = [f_rep[fsrc[4 * half + j, t + k]] for j in range(4)]
                    g = jnp.where(
                        group < 2,
                        jnp.where(group == 0, g[0], g[1]),
                        jnp.where(group == 2, g[2], g[3]),
                    )
                    x.append(halves(g))
                    m = jnp.concatenate([cpl_v[t + k, 4 * half + j] for j in range(4)], axis=1)
                    w.append(halves(m))
                for part_of in range(2):
                    xs.append(jnp.concatenate([v[part_of] for v in x], axis=1))
                    ws.append(jnp.concatenate([v[part_of] for v in w], axis=1))
            r = dot_nt(jnp.concatenate(xs, axis=0), jnp.concatenate(ws, axis=0))
            for k in range(4):
                v = r[32 * k : 32 * k + 32, 64 * k : 64 * k + 64]
                v = v[:COLS] + v[COLS:]
                ll_x[t + k] = coef_form(jnp.concatenate([v[:, :32] + v[:, 32:]] * 4, axis=1))

    root_sends[3].wait_recv()
    x = jnp.concatenate([root_x[...], lrecv[3]], axis=1)
    w = jnp.concatenate(
        [rows_form(*halves(above(n0))), rows_form(*halves(above(n0 + side)))], axis=0
    )
    pair = coef_form(dot_nn(x, w))
    pair_x[...] = pair
    chips[chip] = pair
    chip_sends = [
        pltpu.make_async_remote_copy(
            src_ref=pair_x,
            dst_ref=chips.at[chip],
            send_sem=gs_sem.at[k - 1],
            recv_sem=gr_sem.at[k - 1],
            device_id={"leaf": leaf_at(2 * k)},
            device_id_type=MESH,
        )
        for k in range(1, 32)
    ]

    loads[4].wait()
    loads[5].wait()
    leaf_coupling(0, 8)

    for send in halo_out[:2]:
        send.wait_recv()
    for send in halo_relay:
        send.start()

    pl.semaphore_wait(news.at[1], far_planes)
    for send in chip_sends:
        send.start()

    leaf_coupling(8, 8)

    loads[6].wait()
    loads[7].wait()
    for send in own_out[2:] + own_relay + halo_out[2:] + halo_relay:
        send.wait_recv()

    def near(begin, count):
        @pl.loop(begin, begin + count, unroll=8)
        def _(t):
            x = jnp.concatenate([buf[nsrc[0, t]], buf[nsrc[1, t]]], axis=1)
            w = jnp.concatenate([blk_v[t, 0], blk_v[t, 1]], axis=1)
            o = dot_nt(x, w)
            for q in range(NRHS):
                part[q, t] = o[COLS * q : COLS * (q + 1)]

    def partial(index, dest, t0, count, target, landing):
        return over_rhs(
            part.at[dest, pl.ds(t0, count)], landing, target, ps_sem.at[index], pr_sem.at[index]
        )

    raw_sends = [
        partial(0, across, 0, 8, right, raw.at[0, pl.ds(0, 8)]),
        partial(1, across, 16, 8, left, raw.at[1, pl.ds(0, 8)]),
        partial(2, across, 8, 8, right, raw.at[0, pl.ds(8, 8)]),
        partial(3, across, 24, 8, left, raw.at[1, pl.ds(8, 8)]),
    ]
    plain_sends = [
        partial(4, right, 16, 16, right, rbuf.at[0, upper]),
        partial(5, left, 0, 16, left, rbuf.at[1, lower]),
    ]
    sum_sends = [
        partial(6, right, 0, 8, right, rbuf.at[0, pl.ds(0, 8)]),
        partial(7, left, 16, 8, left, rbuf.at[1, pl.ds(16, 8)]),
        partial(8, right, 8, 8, right, rbuf.at[0, pl.ds(8, 8)]),
        partial(9, left, 24, 8, left, rbuf.at[1, pl.ds(24, 8)]),
    ]
    for i, begin in enumerate((0, 16, 8, 24)):
        near(begin, 8)
        raw_sends[i].start()
    for send in plain_sends:
        send.start()

    def join(i):
        side_of, begin = ((0, 0), (1, 16), (0, 8), (1, 24))[i]
        dest = left if side_of else right
        raw_sends[i].wait_recv()

        @pl.loop(0, 8, unroll=8)
        def _(k):
            t = begin + k
            part[dest, t] = part[dest, t] + raw[side_of, t - 16 * side_of]

        sum_sends[i].start()

    loads[8].wait()
    for c in range(3):
        for a in range(8):
            blk = jnp.concatenate(
                [upc_v[c, pl.ds(8 * b + a, 32, stride=32), :] for b in range(4)], axis=0
            )
            cf[pl.ds(1024 * c + 128 * a, 128), :] = blk.T

    join(0)
    join(1)

    down = None
    couplings = {}
    for level in range(5):
        n = lax.div(n0, 2**level)
        width = NLEAF // 2**level
        t = n - width
        even = lax.rem(t, 2) == 0
        valid = (t >= 2, t + 2 < width, jnp.where(even, t + 3 < width, t >= 3))
        where_to = (n - 2, n + 2, n + 3 - 6 * lax.rem(t, 2))
        cts = []
        for c in range(3):
            ct = unfold(cf[pl.ds(1024 * c + n, 8, stride=128), :])
            cts.append(ct * valid[c].astype(F32))
        if level:
            left_side = jnp.concatenate([coef_form(ct) for ct in cts], axis=0)
            r = dot_nt(left_side, lanes_form(down))
            cts = [r[32 * c : 32 * (c + 1)] for c in range(3)]
        couplings[level] = [
            (jnp.where(ok, place, n), ct) for ok, place, ct in zip(valid, where_to, cts)
        ]
        if level == 0:
            down = above(n0)
        elif level < 4:
            down = dot_nn(coef_form(down), rows_form(*halves(above(n))))

    leaf_coupling(16, 8)

    join(2)
    join(3)

    leaf_coupling(24, 8)

    for n in range(4, 8):
        m_rep[n] = jnp.zeros((32, 128), F32)
    for level in (4, 3, 2, 1):
        width = NLEAF // 2**level
        if level < 4:
            for p in range(width // 2, width):
                lhs = jnp.concatenate(
                    [coef_form(above(2 * p)), coef_form(above(2 * p + 1))], axis=0
                )
                r = dot_nn(lhs, rows_form(*halves(m_rep[p])))
                m_rep[2 * p] = r[:32]
                m_rep[2 * p + 1] = r[32:]
        for place, ct in couplings[level]:
            m_rep[place] = m_rep[place] + ct

    @pl.loop(0, 32, unroll=4)
    def _(e):
        high, low = halves(m_rep[32 + e])
        m_hi[e] = high
        m_lo[e] = low

    for i in range(3):
        pl.when(root_in_ok[i])(root_sends[i].wait_recv)
    field = jnp.zeros((COLS, 128), F32)
    for c in range(3):
        field = field + dot_nn(lrecv[c], rows_form(*halves(couplings[0][c][1])))
    for send in chip_sends:
        send.wait_recv()
    for e in range(0, 32, 2):
        x = jnp.concatenate([chips[e], chips[e + 1]], axis=1)
        w = jnp.concatenate(
            [rows_form(m_hi[e], m_lo[e]), rows_form(m_hi[e + 1], m_lo[e + 1])], axis=0
        )
        field = field + dot_nn(x, w)
    field_x = coef_form(field)

    @pl.loop(0, LEAVES, step=2, unroll=4)
    def _(t):
        x = jnp.concatenate(
            [jnp.concatenate([field_x, ll_x[t + k]], axis=1) for k in range(2)], axis=0
        )
        w = jnp.concatenate(
            [
                jnp.concatenate(
                    [rows_form(q_hi[t + k], q_lo[t + k]), rows_form(b_hi[t + k], b_lo[t + k])],
                    axis=0,
                )
                for k in range(2)
            ],
            axis=1,
        )
        r = dot_nn(x, w)
        for k in range(2):
            acc[t + k] = r[COLS * k : COLS * (k + 1), 128 * k : 128 * (k + 1)]

    for send in plain_sends:
        send.wait_recv()
    for i, begin in enumerate((0, 16, 8, 24)):
        sum_sends[i].wait_recv()

        @pl.loop(begin, begin + 8, unroll=8)
        def _(t):
            near_sum = part[me, t] + (rbuf[0, t] + rbuf[1, t])
            out[:, pl.ds(pl.multiple_of(t * WIDTH, WIDTH), WIDTH)] = near_sum + acc[t]

    for j in range(6):
        pl.when(inside(FACES[j]))(halo_sends[j].wait_send)
    for i in range(3):
        pl.when(root_out_ok[i])(root_sends[i].wait_send)
    for send in root_sends[3:] + own_out + own_relay + halo_out + halo_relay:
        send.wait_send()
    for send in chip_sends + raw_sends + plain_sends + sum_sends:
        send.wait_send()


def local(dens, bases, blocks, near_src, send_leaf, far_src, coupling, local_t, upper_t, up_c):
    any_spec = pl.BlockSpec(memory_space=pltpu.HBM)
    dma = pltpu.SemaphoreType.DMA
    vmem = pltpu.VMEM
    return pl.pallas_call(
        kernel,
        out_shape=jax.ShapeDtypeStruct((COLS, LEAVES * WIDTH), F32),
        in_specs=[any_spec] * 10,
        out_specs=pl.BlockSpec(memory_space=pltpu.VMEM),
        scratch_shapes=[
            pltpu.SMEM((2, LEAVES), jnp.int32),
            pltpu.SMEM((6, 4, NLEAF), jnp.int32),
            pltpu.SMEM((8, LEAVES), jnp.int32),
            vmem((LEAVES, COLS, WIDTH), BF16),
            vmem((SLOTS, NRHS * COLS, WIDTH), BF16),
            vmem((6, 4, COLS, WIDTH), BF16),
            vmem((32, LEAVES * WIDTH), F32),
            vmem((LEAVES, 2, WIDTH, WIDTH), BF16),
            vmem((LEAVES, 8, 32, 32), F32),
            vmem((1024, 64), F32),
            vmem((1024, 128), F32),
            vmem((3, 1024, 128), F32),
            vmem((512, 128), F32),
            vmem((1024, 128), F32),
            vmem((3072, 128), F32),
            vmem((64, 32, 128), BF16),
            vmem((LEAVES, 32, 128), BF16),
            vmem((LEAVES, 32, 128), BF16),
            vmem((LEAVES, 32, 128), BF16),
            vmem((LEAVES, 32, 128), BF16),
            vmem((64, 32, 128), BF16),
            vmem((LEAVES, COLS, 128), F32),
            vmem((LEAVES, COLS, 128), BF16),
            vmem((LEAVES, COLS, 128), F32),
            vmem((64, 32, 128), F32),
            vmem((32, 32, 128), BF16),
            vmem((32, 32, 128), BF16),
            vmem((COLS, 128), BF16),
            vmem((COLS, 128), BF16),
            vmem((4, COLS, 128), BF16),
            vmem((32, COLS, 128), BF16),
            vmem((NRHS, LEAVES, COLS, WIDTH), F32),
            vmem((2, 16, COLS, WIDTH), F32),
            vmem((2, LEAVES, COLS, WIDTH), F32),
            dma((LEAVES,)),
            dma((9,)),
            dma((6,)),
            dma((6,)),
            dma((6,)),
            dma((6,)),
            dma((6,)),
            dma((6,)),
            dma((4,)),
            dma((4,)),
            dma((31,)),
            dma((31,)),
            dma((10,)),
            dma((10,)),
            pltpu.SemaphoreType.REGULAR((2,)),
        ],
        compiler_params=pltpu.CompilerParams(
            collective_id=0, has_side_effects=True, vmem_limit_bytes=48 * 2**20
        ),
        name="h2_product",
    )(
        *(
            pltpu.with_memory_space_constraint(x, pltpu.HBM)
            for x in (
        dens,
        bases,
        blocks,
        near_src.T,
        send_leaf.transpose(1, 2, 0),
        far_src.T,
        coupling,
        local_t[0].transpose(1, 2, 0).reshape(1024, 64),
        upper_t.transpose(1, 2, 0).reshape(1024, 128),
        up_c.transpose(1, 2, 3, 0).reshape(3, 1024, 128),
            )
        )
    )


def solution(mesh):
    in_specs = (
        P("rhs", "leaf"),
        P(None, "leaf"),
        P("leaf", "rhs", None, None),
        P("leaf", "rhs"),
        P(),
        P("leaf", None),
        P("leaf", None, None, None),
        P("leaf", None, None, None),
        P(),
        P(),
    )
    return jax.shard_map(
        local, mesh=mesh, in_specs=in_specs, out_specs=P("rhs", "leaf"), check_vma=False
    )
```

```python
import functools

import jax
import jax.numpy as jnp
from jax import lax
from jax.experimental import pallas as pl
from jax.experimental.pallas import tpu as pltpu
from jax.sharding import PartitionSpec as P

F32 = jnp.float32
BF16 = jnp.bfloat16
MESH = pl.DeviceIdType.MESH
LEAVES = 32
WIDTH = 128
COLS = 16
NLEAF = 64
NRHS = 4
SLOTS = 56
FACES = (1, -1, 4, -4, 16, -16)
VIA_RIGHT = (0, 3, 4)
GREET = tuple(range(1, 9)) + (16, 24)


def dot_nn(a, b):
    return lax.dot_general(a, b, (((1,), (0,)), ((), ())), preferred_element_type=F32)


def dot_nt(a, b):
    return lax.dot_general(a, b, (((1,), (1,)), ((), ())), preferred_element_type=F32)


def halves(x):
    high = x.astype(BF16)
    return high, (x - high.astype(F32)).astype(BF16)


def lane_group(shape):
    return lax.broadcasted_iota(jnp.int32, shape, len(shape) - 1) // 32


def coef_form(r):
    group = lane_group(r.shape)
    high = r.astype(BF16).astype(F32)
    return jnp.where(group % 2 == 0, high, r - high).astype(BF16)


def unfold(tile):
    group = lane_group(tile.shape)
    turned = [tile] + [pltpu.roll(tile, 32 * k, 1) for k in (1, 2, 3)]
    rows = []
    for b in range(4):
        pick = [turned[(g - b) % 4] for g in range(4)]
        rows.append(
            jnp.where(
                group < 2,
                jnp.where(group == 0, pick[0], pick[1]),
                jnp.where(group == 2, pick[2], pick[3]),
            )
        )
    return jnp.concatenate(rows, axis=0)


def rows_form(high, low):
    return jnp.concatenate([high, high, low, low], axis=0)


def lanes_form(m):
    high = m.astype(BF16).astype(F32)
    v = jnp.where(lane_group(m.shape) < 2, high, m - high).astype(BF16)
    return jnp.concatenate([v] * 4, axis=0)


def kernel(
    dens,
    bases,
    blocks,
    nsrc_h,
    sleaf_h,
    fsrc_h,
    coup,
    loc_t,
    up_t,
    up_c,
    out,
    nsrc,
    sleaf,
    fsrc,
    own,
    buf,
    stage,
    bas_v,
    blk_v,
    cpl_v,
    loc_v,
    upt_v,
    upc_v,
    ef,
    uf,
    cf,
    e_v,
    b_hi,
    b_lo,
    q_hi,
    q_lo,
    t_x,
    f_rep,
    ll_x,
    acc,
    m_rep,
    m_hi,
    m_lo,
    root_x,
    pair_x,
    lrecv,
    chips,
    part,
    raw,
    rbuf,
    own_sem,
    loc_sem,
    os_sem,
    or_sem,
    hs_sem,
    hr_sem,
    ys_sem,
    yr_sem,
    ls_sem,
    lr_sem,
    gs_sem,
    gr_sem,
    ps_sem,
    pr_sem,
    news,
):
    d = lax.axis_index("leaf")
    me = lax.axis_index("rhs")

    def leaf_at(offset):
        return lax.rem(d + (offset + 2 * NLEAF), NLEAF)

    def rhs_at(offset):
        return lax.rem(me + offset, NRHS)

    right, across, left = rhs_at(1), rhs_at(2), rhs_at(3)

    def rows_of(r):
        return pl.ds(pl.multiple_of(r * COLS, COLS), COLS)

    my_rows = rows_of(me)

    def inside(offset):
        if offset > 0:
            return d < NLEAF - offset
        return d >= -offset

    ends = (lax.rem(d, 4), lax.rem(lax.div(d, 4), 4), lax.div(d, 16))
    face_out = [ends[j // 2] <= 2 if j % 2 == 0 else ends[j // 2] >= 1 for j in range(6)]
    face_in = [face_out[j + 1 - 2 * (j % 2)] for j in range(6)]

    def greet(sem, offsets):
        count = 0
        for offset in offsets:
            for o in (offset, -offset):
                count = count + jnp.where(inside(o), 1, 0)

                @pl.when(inside(o))
                def _():
                    pl.semaphore_signal(
                        sem, inc=1, device_id={"leaf": d + o}, device_id_type=MESH
                    )

        return count

    for k in range(LEAVES, SLOTS):
        buf[k, my_rows, :] = jnp.zeros((COLS, WIDTH), BF16)

    barrier = pltpu.get_barrier_semaphore()
    for peer in (right, left):
        pl.semaphore_signal(barrier, inc=1, device_id={"rhs": peer}, device_id_type=MESH)
    greeted = greet(barrier, GREET)

    def own_copy(k):
        return pltpu.make_async_copy(
            dens.at[:, pl.ds(pl.multiple_of(k * WIDTH, WIDTH), WIDTH)], own.at[k], own_sem.at[k]
        )

    pairs = (
        (loc_t, loc_v),
        (bases, bas_v),
        (sleaf_h, sleaf),
        (up_t, upt_v),
        (coup, cpl_v),
        (fsrc_h, fsrc),
        (blocks, blk_v),
        (nsrc_h, nsrc),
        (up_c, upc_v),
    )
    loads = [pltpu.make_async_copy(s, v, loc_sem.at[i]) for i, (s, v) in enumerate(pairs)]
    for load in loads[:3]:
        load.start()

    @pl.loop(0, LEAVES)
    def _(k):
        own_copy(k).start()

    for load in loads[3:]:
        load.start()

    loads[0].wait()
    for a in range(8):
        blk = jnp.concatenate([loc_v[pl.ds(32 * (8 * b + a), 32), :] for b in range(4)], axis=0)
        ef[pl.ds(64 * a, 64), :] = blk.T

    @pl.loop(0, 64, unroll=8)
    def _(n):
        m = unfold(ef[pl.ds(n, 8, stride=64), :])
        high = m.astype(BF16).astype(F32)
        e_v[n] = jnp.where(lane_group(m.shape) < 2, high, m - high).astype(BF16)

    row = lax.broadcasted_iota(jnp.int32, (32, 128), 0)
    lane = lax.broadcasted_iota(jnp.int32, (32, 128), 1)
    t_x[1] = jnp.where((lane % 64) == row, 1.0, 0.0).astype(BF16)
    for width in (2, 4, 8, 16, 32):
        for p in range(width // 2, width):
            w = jnp.concatenate([e_v[2 * p], e_v[2 * p + 1]], axis=0)
            r = dot_nt(t_x[p], w)
            t_x[2 * p] = coef_form(jnp.concatenate([r[:, :32]] * 4, axis=1))
            t_x[2 * p + 1] = coef_form(jnp.concatenate([r[:, 32:]] * 4, axis=1))

    @pl.loop(0, LEAVES)
    def _(k):
        own_copy(k).wait()

    loads[2].wait()
    for j in range(6):
        for c in range(4):
            wanted = jnp.maximum(sleaf[j, c, d], 0)
            stage[j, c] = own[wanted]

    @pl.loop(0, LEAVES, unroll=8)
    def _(k):
        buf[k, my_rows, :] = own[k]

    pl.semaphore_wait(barrier, 2 + greeted)

    near_planes = greet(news.at[0], (8, 16, 24))

    side = 1 - 2 * lax.rem(d, 2)
    third = d + 3 * side
    third_ok = (third >= 0) & (third < NLEAF)
    partners = (d + 2, d - 2, third, d + side)
    root_out_ok = (inside(2), inside(-2), third_ok)
    root_in_ok = (inside(-2), inside(2), third_ok)
    root_sends = [
        pltpu.make_async_remote_copy(
            src_ref=root_x,
            dst_ref=lrecv.at[i],
            send_sem=ls_sem.at[i],
            recv_sem=lr_sem.at[i],
            device_id={"leaf": partner},
            device_id_type=MESH,
        )
        for i, partner in enumerate(partners)
    ]
    halo_sends = [
        pltpu.make_async_remote_copy(
            src_ref=stage.at[j],
            dst_ref=buf.at[pl.ds(LEAVES + 4 * j, 4), my_rows, :],
            send_sem=hs_sem.at[j],
            recv_sem=hr_sem.at[j],
            device_id={"leaf": d + FACES[j]},
            device_id_type=MESH,
        )
        for j in range(6)
    ]

    def over_rhs(src, dst, target, ssem, rsem):
        return pltpu.make_async_remote_copy(
            src_ref=src,
            dst_ref=dst,
            send_sem=ssem,
            recv_sem=rsem,
            device_id={"rhs": target},
            device_id_type=MESH,
        )

    def pass_on(slots, target, source, index, ssem, rsem):
        piece = buf.at[slots, rows_of(source), :]
        return over_rhs(piece, piece, target, ssem.at[index], rsem.at[index])

    lower, upper = pl.ds(0, 16), pl.ds(16, 16)
    own_out = [
        over_rhs(own.at[lower], buf.at[lower, my_rows, :], right, os_sem.at[0], or_sem.at[0]),
        over_rhs(own.at[upper], buf.at[upper, my_rows, :], left, os_sem.at[1], or_sem.at[1]),
        over_rhs(own.at[upper], buf.at[upper, my_rows, :], right, os_sem.at[2], or_sem.at[2]),
        over_rhs(own.at[lower], buf.at[lower, my_rows, :], left, os_sem.at[3], or_sem.at[3]),
    ]
    own_relay = [
        pass_on(lower, right, left, 4, os_sem, or_sem),
        pass_on(upper, left, right, 5, os_sem, or_sem),
    ]
    def face_on(j, target, source, index):
        return pass_on(pl.ds(LEAVES + 4 * j, 4), target, source, index, ys_sem, yr_sem)

    halo_right = [face_on(j, right, me, j) for j in range(6)]
    halo_left = [face_on(j, left, me, 6 + j) for j in range(6)]
    halo_relay = [
        face_on(j, right, left, 12 + j) if j in VIA_RIGHT else face_on(j, left, right, 12 + j)
        for j in range(6)
    ]
    halo_first = [halo_right[j] if j in VIA_RIGHT else halo_left[j] for j in range(6)]
    halo_later = [halo_left[j] if j in VIA_RIGHT else halo_right[j] for j in range(6)]
    for j in range(6):
        pl.when(face_out[j])(halo_sends[j].start)
    for send in own_out:
        send.start()

    loads[1].wait()

    @pl.loop(0, LEAVES, step=2, unroll=4)
    def _(t):
        maps = []
        for k in range(2):
            lanes = pl.ds(pl.multiple_of((t + k) * WIDTH, WIDTH), WIDTH)
            b_hi[t + k], b_lo[t + k] = pair = halves(bas_v[:, lanes])
            maps.append(rows_form(*pair))
        x = jnp.concatenate([t_x[LEAVES + t], t_x[LEAVES + t + 1]], axis=0)
        r = dot_nn(x, jnp.concatenate(maps, axis=1))
        for k in range(2):
            q_hi[t + k], q_lo[t + k] = halves(r[32 * k : 32 * k + 32, 128 * k : 128 * k + 128])

    root = jnp.zeros((COLS, 64), F32)
    for t in range(0, LEAVES, 2):
        x = jnp.concatenate([own[t], own[t + 1]], axis=1)
        w = jnp.concatenate(
            [
                jnp.concatenate([q_hi[t], q_hi[t + 1]], axis=1),
                jnp.concatenate([q_lo[t], q_lo[t + 1]], axis=1),
            ],
            axis=0,
        )
        root = root + dot_nt(x, w)
    root = root[:, :32] + root[:, 32:]
    root_x[...] = coef_form(jnp.concatenate([root] * 4, axis=1))
    root_sends[3].start()
    for i in range(3):
        pl.when(root_out_ok[i])(root_sends[i].start)

        @pl.when(jnp.logical_not(root_in_ok[i]))
        def _():
            lrecv[i] = jnp.zeros((COLS, 128), BF16)

    pl.semaphore_wait(news.at[0], near_planes)
    far_planes = greet(news.at[1], (32,))

    @pl.loop(0, LEAVES, step=4, unroll=4)
    def _(t):
        w = jnp.concatenate([m[t + k] for k in range(4) for m in (b_hi, b_lo)], axis=0)
        r = dot_nt(jnp.concatenate([own[t + k] for k in range(4)], axis=0), w)
        for k in range(4):
            v = r[COLS * k : COLS * (k + 1), 64 * k : 64 * (k + 1)]
            f_rep[t + k] = jnp.concatenate([v[:, :32] + v[:, 32:]] * 4, axis=1)

    for j in range(6):
        pl.when(face_in[j])(halo_sends[j].wait_recv)
    for group in (halo_first, halo_later):
        for j in range(6):
            pl.when(face_in[j])(group[j].start)
    for send in own_out[:2]:
        send.wait_recv()
    for send in own_relay:
        send.start()

    loads[3].wait()
    for a in range(8):
        blk = jnp.concatenate([upt_v[pl.ds(32 * (8 * b + a), 32), :] for b in range(4)], axis=0)
        uf[pl.ds(128 * a, 128), :] = blk.T

    def above(n):
        return unfold(uf[pl.ds(n, 8, stride=128), :])

    n0 = d + NLEAF
    chip = lax.div(d, 2)

    def leaf_coupling(begin, count):
        @pl.loop(begin, begin + count, step=4, unroll=2)
        def _(t):
            group = lane_group((COLS, 128))
            xs, ws = [], []
            for k in range(4):
                x, w = [], []
                for half in range(2):
                    g = [f_rep[fsrc[4 * half + j, t + k]] for j in range(4)]
                    g = jnp.where(
                        group < 2,
                        jnp.where(group == 0, g[0], g[1]),
                        jnp.where(group == 2, g[2], g[3]),
                    )
                    x.append(halves(g))
                    m = jnp.concatenate([cpl_v[t + k, 4 * half + j] for j in range(4)], axis=1)
                    w.append(halves(m))
                for part_of in range(2):
                    xs.append(jnp.concatenate([v[part_of] for v in x], axis=1))
                    ws.append(jnp.concatenate([v[part_of] for v in w], axis=1))
            r = dot_nt(jnp.concatenate(xs, axis=0), jnp.concatenate(ws, axis=0))
            for k in range(4):
                v = r[32 * k : 32 * k + 32, 64 * k : 64 * k + 64]
                v = v[:COLS] + v[COLS:]
                ll_x[t + k] = coef_form(jnp.concatenate([v[:, :32] + v[:, 32:]] * 4, axis=1))

    root_sends[3].wait_recv()
    x = jnp.concatenate([root_x[...], lrecv[3]], axis=1)
    w = jnp.concatenate(
        [rows_form(*halves(above(n0))), rows_form(*halves(above(n0 + side)))], axis=0
    )
    pair = coef_form(dot_nn(x, w))
    pair_x[...] = pair
    chips[chip] = pair
    chip_sends = [
        pltpu.make_async_remote_copy(
            src_ref=pair_x,
            dst_ref=chips.at[chip],
            send_sem=gs_sem.at[k - 1],
            recv_sem=gr_sem.at[k - 1],
            device_id={"leaf": leaf_at(2 * k)},
            device_id_type=MESH,
        )
        for k in range(1, 32)
    ]

    loads[4].wait()
    loads[5].wait()
    leaf_coupling(0, 8)

    for j in range(6):

        @pl.when(face_in[j])
        def _():
            halo_first[j].wait_recv()
            halo_relay[j].start()

    pl.semaphore_wait(news.at[1], far_planes)
    for send in chip_sends:
        send.start()

    leaf_coupling(8, 8)

    loads[6].wait()
    loads[7].wait()
    for send in own_out[2:] + own_relay:
        send.wait_recv()
    for j in range(6):

        @pl.when(face_in[j])
        def _():
            halo_later[j].wait_recv()
            halo_relay[j].wait_recv()

    def near(begin, count):
        @pl.loop(begin, begin + count, unroll=8)
        def _(t):
            x = jnp.concatenate([buf[nsrc[0, t]], buf[nsrc[1, t]]], axis=1)
            w = jnp.concatenate([blk_v[t, 0], blk_v[t, 1]], axis=1)
            o = dot_nt(x, w)
            for q in range(NRHS):
                part[q, t] = o[COLS * q : COLS * (q + 1)]

    def partial(index, dest, t0, count, target, landing):
        return over_rhs(
            part.at[dest, pl.ds(t0, count)], landing, target, ps_sem.at[index], pr_sem.at[index]
        )

    raw_sends = [
        partial(0, across, 0, 8, right, raw.at[0, pl.ds(0, 8)]),
        partial(1, across, 16, 8, left, raw.at[1, pl.ds(0, 8)]),
        partial(2, across, 8, 8, right, raw.at[0, pl.ds(8, 8)]),
        partial(3, across, 24, 8, left, raw.at[1, pl.ds(8, 8)]),
    ]
    plain_sends = [
        partial(4, right, 16, 16, right, rbuf.at[0, upper]),
        partial(5, left, 0, 16, left, rbuf.at[1, lower]),
    ]
    sum_sends = [
        partial(6, right, 0, 8, right, rbuf.at[0, pl.ds(0, 8)]),
        partial(7, left, 16, 8, left, rbuf.at[1, pl.ds(16, 8)]),
        partial(8, right, 8, 8, right, rbuf.at[0, pl.ds(8, 8)]),
        partial(9, left, 24, 8, left, rbuf.at[1, pl.ds(24, 8)]),
    ]
    for i, begin in enumerate((0, 16, 8, 24)):
        near(begin, 8)
        raw_sends[i].start()
    for send in plain_sends:
        send.start()

    def join(i):
        side_of, begin = ((0, 0), (1, 16), (0, 8), (1, 24))[i]
        dest = left if side_of else right
        raw_sends[i].wait_recv()

        @pl.loop(0, 8, unroll=8)
        def _(k):
            t = begin + k
            part[dest, t] = part[dest, t] + raw[side_of, t - 16 * side_of]

        sum_sends[i].start()

    loads[8].wait()
    for c in range(3):
        for a in range(8):
            blk = jnp.concatenate(
                [upc_v[c, pl.ds(8 * b + a, 32, stride=32), :] for b in range(4)], axis=0
            )
            cf[pl.ds(1024 * c + 128 * a, 128), :] = blk.T

    join(0)
    join(1)

    down = None
    couplings = {}
    for level in range(5):
        n = lax.div(n0, 2**level)
        width = NLEAF // 2**level
        t = n - width
        even = lax.rem(t, 2) == 0
        valid = (t >= 2, t + 2 < width, jnp.where(even, t + 3 < width, t >= 3))
        where_to = (n - 2, n + 2, n + 3 - 6 * lax.rem(t, 2))
        cts = []
        for c in range(3):
            ct = unfold(cf[pl.ds(1024 * c + n, 8, stride=128), :])
            cts.append(ct * valid[c].astype(F32))
        if level:
            left_side = jnp.concatenate([coef_form(ct) for ct in cts], axis=0)
            r = dot_nt(left_side, lanes_form(down))
            cts = [r[32 * c : 32 * (c + 1)] for c in range(3)]
        couplings[level] = [
            (jnp.where(ok, place, n), ct) for ok, place, ct in zip(valid, where_to, cts)
        ]
        if level == 0:
            down = above(n0)
        elif level < 4:
            down = dot_nn(coef_form(down), rows_form(*halves(above(n))))

    leaf_coupling(16, 8)

    join(2)
    join(3)

    leaf_coupling(24, 8)

    for n in range(4, 8):
        m_rep[n] = jnp.zeros((32, 128), F32)
    for level in (4, 3, 2, 1):
        width = NLEAF // 2**level
        if level < 4:
            for p in range(width // 2, width):
                lhs = jnp.concatenate(
                    [coef_form(above(2 * p)), coef_form(above(2 * p + 1))], axis=0
                )
                r = dot_nn(lhs, rows_form(*halves(m_rep[p])))
                m_rep[2 * p] = r[:32]
                m_rep[2 * p + 1] = r[32:]
        for place, ct in couplings[level]:
            m_rep[place] = m_rep[place] + ct

    @pl.loop(0, 32, unroll=4)
    def _(e):
        high, low = halves(m_rep[32 + e])
        m_hi[e] = high
        m_lo[e] = low

    for i in range(3):
        pl.when(root_in_ok[i])(root_sends[i].wait_recv)
    field = jnp.zeros((COLS, 128), F32)
    for c in range(3):
        field = field + dot_nn(lrecv[c], rows_form(*halves(couplings[0][c][1])))
    for send in chip_sends:
        send.wait_recv()
    for e in range(0, 32, 2):
        x = jnp.concatenate([chips[e], chips[e + 1]], axis=1)
        w = jnp.concatenate(
            [rows_form(m_hi[e], m_lo[e]), rows_form(m_hi[e + 1], m_lo[e + 1])], axis=0
        )
        field = field + dot_nn(x, w)
    field_x = coef_form(field)

    @pl.loop(0, LEAVES, step=2, unroll=4)
    def _(t):
        x = jnp.concatenate(
            [jnp.concatenate([field_x, ll_x[t + k]], axis=1) for k in range(2)], axis=0
        )
        w = jnp.concatenate(
            [
                jnp.concatenate(
                    [rows_form(q_hi[t + k], q_lo[t + k]), rows_form(b_hi[t + k], b_lo[t + k])],
                    axis=0,
                )
                for k in range(2)
            ],
            axis=1,
        )
        r = dot_nn(x, w)
        for k in range(2):
            acc[t + k] = r[COLS * k : COLS * (k + 1), 128 * k : 128 * (k + 1)]

    for send in plain_sends:
        send.wait_recv()
    for i, begin in enumerate((0, 16, 8, 24)):
        sum_sends[i].wait_recv()

        @pl.loop(begin, begin + 8, unroll=8)
        def _(t):
            near_sum = part[me, t] + (rbuf[0, t] + rbuf[1, t])
            out[:, pl.ds(pl.multiple_of(t * WIDTH, WIDTH), WIDTH)] = near_sum + acc[t]

    for j in range(6):
        pl.when(face_out[j])(halo_sends[j].wait_send)

        @pl.when(face_in[j])
        def _():
            for send in (halo_right[j], halo_left[j], halo_relay[j]):
                send.wait_send()

    for i in range(3):
        pl.when(root_out_ok[i])(root_sends[i].wait_send)
    for send in root_sends[3:] + own_out + own_relay:
        send.wait_send()
    for send in chip_sends + raw_sends + plain_sends + sum_sends:
        send.wait_send()


def local(dens, bases, blocks, near_src, send_leaf, far_src, coupling, local_t, upper_t, up_c):
    any_spec = pl.BlockSpec(memory_space=pltpu.HBM)
    dma = pltpu.SemaphoreType.DMA
    vmem = pltpu.VMEM
    return pl.pallas_call(
        kernel,
        out_shape=jax.ShapeDtypeStruct((COLS, LEAVES * WIDTH), F32),
        in_specs=[any_spec] * 10,
        out_specs=pl.BlockSpec(memory_space=pltpu.VMEM),
        scratch_shapes=[
            pltpu.SMEM((2, LEAVES), jnp.int32),
            pltpu.SMEM((6, 4, NLEAF), jnp.int32),
            pltpu.SMEM((8, LEAVES), jnp.int32),
            vmem((LEAVES, COLS, WIDTH), BF16),
            vmem((SLOTS, NRHS * COLS, WIDTH), BF16),
            vmem((6, 4, COLS, WIDTH), BF16),
            vmem((32, LEAVES * WIDTH), F32),
            vmem((LEAVES, 2, WIDTH, WIDTH), BF16),
            vmem((LEAVES, 8, 32, 32), F32),
            vmem((1024, 64), F32),
            vmem((1024, 128), F32),
            vmem((3, 1024, 128), F32),
            vmem((512, 128), F32),
            vmem((1024, 128), F32),
            vmem((3072, 128), F32),
            vmem((64, 32, 128), BF16),
            vmem((LEAVES, 32, 128), BF16),
            vmem((LEAVES, 32, 128), BF16),
            vmem((LEAVES, 32, 128), BF16),
            vmem((LEAVES, 32, 128), BF16),
            vmem((64, 32, 128), BF16),
            vmem((LEAVES, COLS, 128), F32),
            vmem((LEAVES, COLS, 128), BF16),
            vmem((LEAVES, COLS, 128), F32),
            vmem((64, 32, 128), F32),
            vmem((32, 32, 128), BF16),
            vmem((32, 32, 128), BF16),
            vmem((COLS, 128), BF16),
            vmem((COLS, 128), BF16),
            vmem((4, COLS, 128), BF16),
            vmem((32, COLS, 128), BF16),
            vmem((NRHS, LEAVES, COLS, WIDTH), F32),
            vmem((2, 16, COLS, WIDTH), F32),
            vmem((2, LEAVES, COLS, WIDTH), F32),
            dma((LEAVES,)),
            dma((9,)),
            dma((6,)),
            dma((6,)),
            dma((6,)),
            dma((6,)),
            dma((18,)),
            dma((18,)),
            dma((4,)),
            dma((4,)),
            dma((31,)),
            dma((31,)),
            dma((10,)),
            dma((10,)),
            pltpu.SemaphoreType.REGULAR((2,)),
        ],
        compiler_params=pltpu.CompilerParams(
            collective_id=0, has_side_effects=True, vmem_limit_bytes=48 * 2**20
        ),
        name="h2_product",
    )(
        *(
            pltpu.with_memory_space_constraint(x, pltpu.HBM)
            for x in (
        dens,
        bases,
        blocks,
        near_src.T,
        send_leaf.transpose(1, 2, 0),
        far_src.T,
        coupling,
        local_t[0].transpose(1, 2, 0).reshape(1024, 64),
        upper_t.transpose(1, 2, 0).reshape(1024, 128),
        up_c.transpose(1, 2, 3, 0).reshape(3, 1024, 128),
            )
        )
    )


def solution(mesh):
    in_specs = (
        P("rhs", "leaf"),
        P(None, "leaf"),
        P("leaf", "rhs", None, None),
        P("leaf", "rhs"),
        P(),
        P("leaf", None),
        P("leaf", None, None, None),
        P("leaf", None, None, None),
        P(),
        P(),
    )
    return jax.shard_map(
        local, mesh=mesh, in_specs=in_specs, out_specs=P("rhs", "leaf"), check_vma=False
    )
```
